32 devices in a mesh: stator: 8 (over z, y), axial: 4 (over x, core).
Axes of the slice: x: 2, y: 2, z: 4, core: 2. Of those that a mesh axis runs over, the one named last changes fastest.
Arguments:
- coeffs: float32 [32, 32768], P(None, ('stator', 'axial')), may hold values from -6 to 6
- elem_edge: int32 [6, 32768], P(None, ('stator', 'axial')), may hold values from 0 to 1151
- curl_map: float32 [3, 6, 32768], P(None, None, ('stator', 'axial')), may hold values from -1.8 to 1.8
- jacobian: bfloat16 [6, 32, 32768], P(None, None, ('stator', 'axial')), may hold values from -4 to 10, as said below
- flux_fwd: bfloat16 [3, 32, 32768], P(None, None, ('stator', 'axial')), may hold values from -6 to 6
- density: float32 [32768], P(('stator', 'axial')), may hold values from 0.05 to 1
- mortar: float32 [128, 128], replicated, may hold values from -0.5 to 0.5
- gap_peer: int32 [4096, 1], P(('stator', 'axial')), may hold values from 0 to 7; in each aligned block of 128 rows (0 to 127, 128 to 255, ...) at most 32 rows name the same one
- gap_block: int32 [4096], P(('stator', 'axial')), may hold values from 0 to 1
Outputs:
- adjoint: float32 [32, 32768], P(None, ('stator', 'axial'))
- density_grad: float32 [32768], P(('stator', 'axial'))
The draws below stay inside these ranges and needn't reach their ends.
Inputs may be any that keep to these rules, and one draw needn't show every extreme that they name: `elem_edge`: each entry indexes the device's own 1024 edges followed by the first 128 edges of the next axial slab. `gap_peer`: row s * 4 + b of one device names the stator index whose face meets rotor face block b at sample s; at most 32 rows of one device name the same index, and exactly 32 for some index. `jacobian`: each sample's six components form a symmetric matrix with positive diagonal; each off-diagonal entry is at most 0.41 times the square root of the product of its two diagonal entries, so the matrix is positive definite.
All inputs are finite; a program needn't handle non-finite values.
Results may differ from the reference program's by a relative error of at most 0.0003.
Values sent between devices are 32-bit elements; how exact they have to be, the bound alone decides.
No kernel may reach another device: no remote copies, remote signals or barrier semaphores. Data moves between devices by JAX's collectives and lax.ppermute only.
A program may use at most 64 MiB of HBM per device.

```python
import math
import jax
import jax.numpy as jnp
import numpy as np
from jax import lax

S = 32
EDGE_DEV = 1024
ELEM_DEV = 1024
FACE = 128
GE = 128
GB = 4
QB = 2
CAP = 32
EDGES = 32768
ELEMS = 32768
N_STATOR = 8
N_AXIAL = 4


def draw_jacobian(key, part):
    first_key, second_key = jax.random.split(jax.random.fold_in(key, 17))
    diagonal = jnp.exp(jax.random.uniform(first_key, (3, S, ELEMS), jnp.float32, 0.0, math.log(10.0)))
    spread = jnp.clip(jax.random.normal(second_key, (3, S, ELEMS), jnp.float32) * 0.2, -0.4, 0.4)
    pairs = jnp.stack([jnp.sqrt(diagonal[0] * diagonal[1]), jnp.sqrt(diagonal[0] * diagonal[2]), jnp.sqrt(diagonal[1] * diagonal[2])])
    return jnp.concatenate([diagonal, spread * pairs], 0).astype(jnp.bfloat16)


def place_ends(result, rng, least, high):
    longest = result.shape.index(max(result.shape))
    spots = []
    for shift in (0, 1):
        where = [jax.random.randint(jax.random.fold_in(rng, axis), (), 0, length) for axis, length in enumerate(result.shape)]
        where[longest] = (where[longest] + shift) % result.shape[longest]
        spots.append(tuple(where))
    return result.at[spots[0]].set(least).at[spots[1]].set(high)


def shard_levels(rng, dims, cuts, low, top_value):
    gain = 1.0
    for dim, shards_of in cuts:
        heights = jax.random.uniform(jax.random.fold_in(jax.random.fold_in(rng, 6), dim), (shards_of,), jnp.float32, low / len(cuts), top_value / len(cuts))
        gain = gain * jnp.repeat(jnp.exp(heights), dims[dim] // shards_of).reshape((-1,) + (1,) * (len(dims) - 1 - dim))
    return gain


def assign_block(rng, own, number, rows, count, top, bound, slope):
    sequence = jax.random.permutation(rng, count)
    heavy_load, common = shares(count, rows * top, bound, slope, True), shares(count, rows * top, bound, slope, False)
    places = jnp.arange(count)

    def named(sizes, turn):
        used = int((sizes > 0).sum())
        fixed = max(1, used // 4)
        moved = fixed + (places - fixed + turn * (used - fixed)) % max(1, count - fixed)
        return jnp.zeros((count,), jnp.int32).at[sequence[jnp.where(places < fixed, places, moved)]].set(jnp.asarray(sizes, jnp.int32))

    sizes = jnp.where(number % 4 == 0, named(heavy_load, number // 4), named(common, number - number // 4 - 1))
    mixed = jax.random.permutation(jax.random.fold_in(own, 3), count)
    source_of, taker = mixed[0:count // 2 * 2:2], mixed[1:count // 2 * 2:2]
    margin = jnp.minimum(sizes[source_of] - 1, bound - sizes[taker]) // 2
    margin = jnp.where((source_of == sequence[0]) | (taker == sequence[0]) | (sizes[taker] == 0), 0, jnp.maximum(margin, 0))
    moved = jax.random.randint(jax.random.fold_in(own, 4), (count // 2,), 0, 1 << 20) % (margin + 1)
    sizes = sizes.at[source_of].add(-moved).at[taker].add(moved)
    labels = jnp.searchsorted(jnp.cumsum(sizes), jnp.arange(rows * top), side="right").astype(jnp.int32)
    listing = labels.reshape(top, rows).T
    listing = listing[jax.random.permutation(jax.random.fold_in(own, 1), rows)]
    turn = jax.random.randint(jax.random.fold_in(own, 2), (rows, 1), 0, top)
    return jnp.take_along_axis(listing, (jnp.arange(top)[None, :] + turn) % top, axis=1)


def shares(count, total, most, slope, full):
    weights = [(1 << 20) // math.isqrt(standing ** slope) + 1 for standing in range(1, count + 1)]
    largest = most if full else min(most, max(-(-total // count), total * weights[0] // sum(weights)))
    least = 1 if total - largest >= count - 1 else 0
    counts, surplus = [largest] + [least] * (count - 1), total - largest - least * (count - 1)
    while surplus > 0:
        movable = [i for i in range(1, count) if counts[i] < largest] or [i for i in range(1, count) if counts[i] < most]
        pool, left = sum([weights[i] for i in movable]), surplus
        for i in movable:
            more = min(most - counts[i], max(1, left * weights[i] // pool), surplus)
            counts[i] = counts[i] + more
            surplus = surplus - more
    return np.array(counts)


def bell_draw(rng, dims, deviation, bound, cuts=(), kind=jnp.bfloat16):
    result = deviation * jax.random.normal(rng, dims, jnp.float32)
    if cuts:
        result = result * shard_levels(rng, dims, cuts, -0.22, 0.18)
    return jnp.clip(result, -bound, bound).astype(kind)


def setup_inputs(seed: int = 0) -> dict:
    arg_keys = jax.random.split(jax.random.key(seed), 10)
    coeffs = bell_draw(arg_keys[0], (S, EDGES), 1.0, 6.0, ((1, 32),), jnp.float32)
    elem_edge = place_ends(jax.random.randint(arg_keys[1], (6, ELEMS), 0, EDGE_DEV + FACE), jax.random.fold_in(arg_keys[1], 1), 0, (EDGE_DEV + FACE) - 1).astype(jnp.int32)
    curl_map = bell_draw(arg_keys[2], (3, 6, ELEMS), 0.3, 1.8, ((2, 32),), jnp.float32)
    jacobian = draw_jacobian(jax.random.fold_in(arg_keys[9], 71), 0)
    flux_fwd = bell_draw(arg_keys[4], (3, S, ELEMS), 1.0, 6.0, ((2, 32),))
    density = jnp.clip(0.05 + 0.95 * jax.random.uniform(arg_keys[5], (ELEMS,), jnp.float32) ** shard_levels(arg_keys[5], (ELEMS,), ((0, 32),), -0.2, 0.2), 0.05, 1.0)
    mortar = bell_draw(arg_keys[6], (GE, GE), GE ** -0.5, 0.5, (), jnp.float32)
    gap_peer_keys = jax.random.split(jax.random.fold_in(arg_keys[7], 1), (N_STATOR * N_AXIAL * S * GB) // (S * GB))
    gap_peer_turns = jax.random.permutation(jax.random.fold_in(arg_keys[7], 3), (N_STATOR * N_AXIAL * S * GB) // (S * GB))
    gap_peer = jax.vmap(lambda own, number: assign_block(jax.random.fold_in(arg_keys[7], 2), own, number, S * GB, N_STATOR, 1, CAP, 2))(gap_peer_keys, gap_peer_turns).reshape((N_STATOR * N_AXIAL * S * GB, 1))
    gap_block = place_ends(jax.random.randint(arg_keys[8], (N_STATOR * N_AXIAL * S * GB,), 0, QB), jax.random.fold_in(arg_keys[8], 1), 0, QB - 1).astype(jnp.int32)
    return {"coeffs": coeffs, "elem_edge": elem_edge, "curl_map": curl_map, "jacobian": jacobian, "flux_fwd": flux_fwd, "density": density, "mortar": mortar, "gap_peer": gap_peer, "gap_block": gap_block}


PENALTY = 4.0
SIMP_POWER = 3.0

def dft_table(count):
    rows = jnp.arange(count, dtype=jnp.float32)[:, None]
    index = jnp.arange(count, dtype=jnp.int32)
    harmonic = ((index + 1) // 2).astype(jnp.float32)[None, :]
    is_sine = ((index % 2 == 0) & (index > 0))[None, :]
    angle = 2.0 * math.pi * harmonic * rows / count
    table = jnp.where(is_sine, jnp.sin(angle), jnp.cos(angle))
    return table * jnp.float32(math.sqrt(2.0 / count))

def element_work(extended, elem_edge, curl_map, jacobian, flux_fwd, density):
    samples = extended.shape[0]
    values = extended[:, elem_edge]
    flux_lam = jnp.einsum('cke,ske->cse', curl_map, values, precision=lax.Precision.HIGHEST)
    jac = jacobian.astype(jnp.float32)
    field_h = jnp.stack([jac[0] * flux_lam[0] + jac[3] * flux_lam[1] + jac[4] * flux_lam[2], jac[3] * flux_lam[0] + jac[1] * flux_lam[1] + jac[5] * flux_lam[2], jac[4] * flux_lam[0] + jac[5] * flux_lam[1] + jac[2] * flux_lam[2]])
    element_terms = jnp.einsum('cke,cse->kes', curl_map, field_h, precision=lax.Precision.HIGHEST)
    summed = jax.ops.segment_sum(element_terms.reshape(-1, samples), elem_edge.reshape(-1), num_segments=extended.shape[1])
    energy = lax.optimization_barrier(jnp.sum(flux_lam * flux_fwd.astype(jnp.float32), axis=(0, 1)))
    grad = SIMP_POWER * density * density * energy / samples
    return (summed.T, grad)

def reference(coeffs, elem_edge, curl_map, jacobian, flux_fwd, density, mortar, gap_peer, gap_block):
    devices = N_STATOR * N_AXIAL
    table = dft_table(S)
    in_time = jnp.dot(table, coeffs, precision=lax.Precision.HIGHEST)
    grid = in_time.reshape(S, N_STATOR, N_AXIAL, EDGE_DEV)
    upper_rim = jnp.concatenate([grid[:, :, 1:, :FACE], jnp.zeros((S, N_STATOR, 1, FACE), jnp.float32)], 2)
    extended = jnp.concatenate([grid, upper_rim], 3).transpose(1, 2, 0, 3).reshape(devices, S, EDGE_DEV + FACE)

    def one_device(device):

        def cols(arr):
            return lax.dynamic_slice_in_dim(arr, device * ELEM_DEV, ELEM_DEV, arr.ndim - 1)
        return element_work(extended[device], cols(elem_edge), cols(curl_map), cols(jacobian), cols(flux_fwd), cols(density))
    res_ext, grads = lax.map(one_device, jnp.arange(devices, dtype=jnp.int32))
    res_ext = res_ext.reshape(N_STATOR, N_AXIAL, S, EDGE_DEV + FACE)
    own = res_ext[..., :EDGE_DEV]
    rim = res_ext[..., EDGE_DEV:]
    own = own.at[:, 1:, :, :FACE].add(rim[:, :-1])
    rotor = grid[..., EDGE_DEV - GB * GE:].reshape(S, N_STATOR, N_AXIAL, GB, GE).transpose(1, 2, 0, 3, 4)
    stator = grid[..., FACE:FACE + QB * GE].reshape(S, N_STATOR, N_AXIAL, QB, GE).transpose(1, 2, 0, 3, 4)
    mapped = jnp.einsum('nasqg,gh->nasqh', stator, mortar, precision=lax.Precision.HIGHEST)
    owners = gap_peer[:, 0].reshape(N_STATOR, N_AXIAL, S, GB)
    blocks = gap_block.reshape(N_STATOR, N_AXIAL, S, GB)
    axial_idx = jnp.broadcast_to(jnp.arange(N_AXIAL, dtype=jnp.int32)[None, :, None, None], owners.shape)
    sample_idx = jnp.broadcast_to(jnp.arange(S, dtype=jnp.int32)[None, None, :, None], owners.shape)
    facing = mapped[owners, axial_idx, sample_idx, blocks]
    jumps = rotor - facing
    gathered = jnp.zeros((N_STATOR, N_AXIAL, S, QB, GE), jnp.float32).at[owners, axial_idx, sample_idx, blocks].add(jumps)
    stator_terms = -PENALTY * jnp.einsum('nasqg,hg->nasqh', gathered, mortar, precision=lax.Precision.HIGHEST)
    own = own.at[..., EDGE_DEV - GB * GE:].add(PENALTY * jumps.reshape(N_STATOR, N_AXIAL, S, GB * GE))
    own = own.at[..., FACE:FACE + QB * GE].add(stator_terms.reshape(N_STATOR, N_AXIAL, S, QB * GE))
    residual = own.transpose(2, 0, 1, 3).reshape(S, devices * EDGE_DEV)
    adjoint = jnp.dot(table.T, residual, precision=lax.Precision.HIGHEST)
    return (adjoint, grads.reshape(-1))
```

```python
import functools
import math

import jax
import jax.numpy as jnp
import numpy as np
from jax import lax
from jax.experimental import pallas as pl
from jax.experimental.pallas import tpu as pltpu
from jax.sharding import PartitionSpec as P

GE = 128
QB = 2
LANES = 128
WIDE = 256
KEY_ROWS = 8

PENALTY = 4.0
SIMP_POWER = 3.0

BF = jnp.bfloat16
F32 = jnp.float32


def shifted(value, axis, steps):
    count = lax.axis_size(axis)
    leading, last = (max(0, -steps), min(count, count - steps))
    return lax.ppermute(value, axis, [(source, source + steps) for source in range(leading, last)])


def dft_table(count):
    rows = np.arange(count, dtype=np.float64)[:, None]
    index = np.arange(count)
    harmonic = ((index + 1) // 2)[None, :]
    is_sine = ((index % 2 == 0) & (index > 0))[None, :]
    angle = 2.0 * math.pi * harmonic * rows / count
    return np.where(is_sine, np.sin(angle), np.cos(angle)) * math.sqrt(2.0 / count)


def table_parts(table):
    high = table.astype(BF)
    low = (table - high.astype(np.float64)).astype(BF)
    return np.concatenate([high, high, low, low], 1)


def split(value):
    high = value.astype(BF)
    low = (value - high.astype(F32)).astype(BF)
    return high, low


def dot(left, right):
    return jnp.dot(left, right, preferred_element_type=F32)


def dot_t(left, right):
    return lax.dot_general(left, right, (((1,), (1,)), ((), ())), preferred_element_type=F32)


def apply_table(table, value):
    high, low = split(value)
    return dot(table, jnp.concatenate([high, low, high, low], 0))


def iota(shape, dim):
    return lax.broadcasted_iota(jnp.int32, shape, dim)


def sorted_rows(peer_ref, block_ref, samples, blocks):
    rows = samples * blocks
    old, new = iota((rows, rows), 0), iota((rows, rows), 1)
    move = jnp.where(old == (new % samples) * blocks + new // samples, 1.0, 0.0).astype(BF)
    both = jnp.concatenate([peer_ref[...], block_ref[...]], 0).astype(F32)
    both = jnp.concatenate([both, jnp.zeros((6, rows), F32)], 0).astype(BF)
    moved = dot(both, move)
    return moved[0:1], moved[1:2]


def gap_kernel(
    samples, stators, blocks, face, rotor_start, table_ref, coeffs_ref, mortar_ref, peer_ref, block_ref,
    send_ref, mapped_ref,
):
    rows = samples * blocks
    slots = 2 * rows
    capacity = slots // stators
    table = table_ref[...]
    face_time = apply_table(table, coeffs_ref[:, face : face + QB * GE])
    rotor_time = apply_table(table, coeffs_ref[:, rotor_start : rotor_start + blocks * GE])
    faces = jnp.concatenate([face_time[:, q * GE : (q + 1) * GE] for q in range(QB)], 0)
    rotors = jnp.concatenate([rotor_time[:, b * GE : (b + 1) * GE] for b in range(blocks)], 0)
    mortar_high, mortar_low = split(mortar_ref[...])
    face_high, face_low = split(faces)
    mapped = dot(
        jnp.concatenate([face_high, face_low, face_high], 1),
        jnp.concatenate([mortar_high, mortar_high, mortar_low], 0),
    )
    mapped_ref[...] = mapped
    peers, chosen = sorted_rows(peer_ref, block_ref, samples, blocks)
    across = jnp.broadcast_to(peers, (rows, rows))
    down = jnp.transpose(across)
    ahead = (across == down) & (iota((rows, rows), 0) < iota((rows, rows), 1))
    rank = jnp.sum(jnp.where(ahead, 1.0, 0.0), 0, keepdims=True)
    place = peers * capacity + rank
    slot = iota((slots, rows), 0).astype(F32)
    pick = jnp.where(slot == place, 1.0, 0.0).astype(BF)
    rotor_high, rotor_low = split(rotors)
    picked = dot(pick, jnp.concatenate([rotor_high, rotor_low], 1))
    packed = picked[:, :GE] + picked[:, GE:]
    key = chosen * samples + (iota((1, rows), 1) % samples).astype(F32) + 1.0
    keys = dot_t(jnp.broadcast_to(key, (KEY_ROWS, rows)).astype(BF), pick)
    for p in range(stators):
        send_ref[p, 0:capacity, :] = packed[p * capacity : (p + 1) * capacity]
        start = p * capacity
        part = keys[:, start // LANES * LANES : (start // LANES + 1) * LANES]
        turn = (LANES - start % LANES) % LANES
        if turn:
            part = pltpu.roll(part, turn, 1)
        send_ref[p, capacity : capacity + KEY_ROWS, :] = part
        send_ref[p, capacity + KEY_ROWS :, :] = mapped


def element_kernel(
    face, rotor_start, table_ref, back_ref, coeffs_ref, rim_ref, edge_ref, curl_ref, jac_ref, fwd_ref, density_ref,
    adjoint_ref, rim_out_ref, grad_ref,
):
    samples, edges = coeffs_ref.shape
    elements = edge_ref.shape[1]
    table = table_ref[...]
    own_time = apply_table(table, coeffs_ref[...])
    rim_time = apply_table(table, rim_ref[...])
    extended = [own_time[:, i * LANES : (i + 1) * LANES] for i in range(edges // LANES)]
    extended += [rim_time[:, i * LANES : (i + 1) * LANES] for i in range(face // LANES)]
    total = edges + face
    wides = -(-total // WIDE)
    places = iota((WIDE, LANES), 0).astype(F32).astype(BF)
    summed = jnp.zeros((wides * 2 * samples, WIDE), F32)
    for chunk in range(elements // WIDE):
        lefts, rights = [], []
        left_lanes = [[] for _ in range(6)]
        right_lanes = [[] for _ in range(6)]
        for half in range(WIDE // LANES):
            start = chunk * WIDE + half * LANES
            lanes = slice(start, start + LANES)
            values = []
            index_rows = edge_ref[:, lanes]
            for m in range(6):
                index = index_rows[m : m + 1]
                low = jnp.broadcast_to(index & (LANES - 1), (samples, LANES))
                high = jnp.broadcast_to(index // LANES, (samples, LANES))
                found = [
                    jnp.take_along_axis(part, low, axis=1, mode="promise_in_bounds") for part in extended
                ]
                bit = 1
                while len(found) > 1:
                    odd = (high & bit) != 0
                    found = [
                        jnp.where(odd, found[i + 1], found[i]) if i + 1 < len(found) else found[i]
                        for i in range(0, len(found), 2)
                    ]
                    bit *= 2
                values.append(found[0])
            curl = [[curl_ref[c, m : m + 1, lanes] for m in range(6)] for c in range(3)]
            flux = []
            for c in range(3):
                acc = curl[c][0] * values[0]
                for m in range(1, 6):
                    acc = acc + curl[c][m] * values[m]
                flux.append(acc)
            energy = flux[0] * fwd_ref[0, :, lanes].astype(F32)
            for c in range(1, 3):
                energy = energy + flux[c] * fwd_ref[c, :, lanes].astype(F32)
            energy = jnp.sum(energy, 0, keepdims=True)
            density = density_ref[:, lanes]
            grad_ref[:, lanes] = SIMP_POWER * density * density * energy / samples
            jac = [jac_ref[k, :, lanes].astype(F32) for k in range(6)]
            field = [
                jac[0] * flux[0] + jac[3] * flux[1] + jac[4] * flux[2],
                jac[3] * flux[0] + jac[1] * flux[1] + jac[5] * flux[2],
                jac[4] * flux[0] + jac[5] * flux[1] + jac[2] * flux[2],
            ]
            for m in range(6):
                term = curl[0][m] * field[0] + curl[1][m] * field[1] + curl[2][m] * field[2]
                high, low = split(term)
                pair = jnp.concatenate([high, low], 0)
                index = index_rows[m : m + 1]
                wide = jnp.broadcast_to(index // WIDE, (16, LANES)).astype(F32).astype(BF)
                wide = jnp.concatenate([wide] * (2 * samples // 16), 0)
                left_lanes[m].append(
                    jnp.concatenate([jnp.where(wide == w, pair, jnp.zeros_like(pair)) for w in range(wides)], 0)
                )
                place = jnp.broadcast_to(index & (WIDE - 1), (16, LANES)).astype(F32).astype(BF)
                place = jnp.concatenate([place] * (WIDE // 16), 0)
                right_lanes[m].append(jnp.where(place == places, jnp.ones_like(place), jnp.zeros_like(place)))
        left = jnp.concatenate([part for m in range(6) for part in left_lanes[m]], 1)
        right = jnp.concatenate([part for m in range(6) for part in right_lanes[m]], 1)
        summed = summed + dot_t(left, right)
    pieces = []
    for w in range(wides):
        base = w * 2 * samples
        pieces.append(summed[base : base + samples] + summed[base + samples : base + 2 * samples])
    residual = jnp.concatenate(pieces, 1)
    own = jnp.concatenate(
        [residual[:, :rotor_start], residual[:, rotor_start:edges] + PENALTY * own_time[:, rotor_start:]], 1
    )
    back = back_ref[...]
    adjoint_ref[...] = apply_table(back, own)
    rim_out_ref[...] = apply_table(back, residual[:, edges:total])


def join_kernel(
    samples, stators, blocks, face, rotor_start, back_ref, adjoint_ref, rim_ref, got_ref, mapped_ref, mortar_ref,
    peer_ref, block_ref, out_ref,
):
    rows = samples * blocks
    slots = 2 * rows
    capacity = slots // stators
    faces_at = capacity + KEY_ROWS
    peers, chosen = sorted_rows(peer_ref, block_ref, samples, blocks)
    wanted = (peers * QB + chosen) * samples + (iota((1, rows), 1) % samples).astype(F32)
    wanted = jnp.transpose(jnp.broadcast_to(wanted, (LANES, rows)))
    face_rows = stators * QB * samples
    select = jnp.concatenate(
        [
            jnp.where(wanted == (iota((rows, LANES), 1) + at).astype(F32), 1.0, 0.0).astype(BF)
            for at in range(0, face_rows, LANES)
        ],
        1,
    )
    faces = jnp.concatenate([got_ref[p, faces_at:, :] for p in range(stators)], 0)
    face_high, face_low = split(faces)
    facing = dot(select, jnp.concatenate([face_high, face_low], 1))
    facing = facing[:, :GE] + facing[:, GE:]
    rotor_term = jnp.concatenate(
        [facing[b * samples : (b + 1) * samples] for b in range(blocks)], 1
    ) * (-PENALTY)

    lane = iota((KEY_ROWS, LANES), 1)
    key_parts = []
    for v in range(slots // LANES):
        acc = jnp.zeros((KEY_ROWS, LANES), F32)
        for p in range(v * LANES // capacity, (v + 1) * LANES // capacity):
            part = jnp.where(lane < capacity, got_ref[p, capacity:faces_at, :], 0.0)
            turn = p * capacity % LANES
            acc = acc + (pltpu.roll(part, turn, 1) if turn else part)
        key_parts.append(acc[0:1])
    key = jnp.concatenate(key_parts, 1)
    targets = QB * samples
    hit = jnp.where(key == (iota((targets, slots), 0) + 1).astype(F32), 1.0, 0.0)
    count = jnp.sum(hit, 1, keepdims=True)
    packed = jnp.concatenate([got_ref[p, 0:capacity, :] for p in range(stators)], 0)
    packed_high, packed_low = split(packed)
    gathered = dot(hit.astype(BF), jnp.concatenate([packed_high, packed_low], 1))
    gathered = gathered[:, :GE] + gathered[:, GE:] - count * mapped_ref[...]
    mortar_high, mortar_low = split(mortar_ref[...])
    gathered_high, gathered_low = split(gathered)
    stator_term = dot_t(
        jnp.concatenate([gathered_high, gathered_low, gathered_high], 1),
        jnp.concatenate([mortar_high, mortar_high, mortar_low], 1),
    ) * (-PENALTY)
    stator_term = jnp.concatenate([stator_term[q * samples : (q + 1) * samples] for q in range(QB)], 1)
    back = back_ref[...]
    out_ref[...] = adjoint_ref[...]
    out_ref[:, :face] += rim_ref[...]
    out_ref[:, face : face + QB * GE] += apply_table(back, stator_term)
    out_ref[:, rotor_start : rotor_start + blocks * GE] += apply_table(back, rotor_term)


def on_device(coeffs, elem_edge, curl_map, jacobian, flux_fwd, density, mortar, gap_peer, gap_block):
    stators = lax.axis_size("stator")
    samples, edges = coeffs.shape
    rows = gap_block.shape[0]
    blocks = rows // samples
    capacity = 2 * rows // stators
    face = edges // 8
    rotor_start = edges - blocks * GE
    elements = density.shape[0]
    table_value = dft_table(samples)
    table = jnp.asarray(table_parts(table_value))
    back = jnp.asarray(table_parts(table_value.T))
    peer = gap_peer.reshape(1, rows)
    block = gap_block.reshape(1, rows)

    rim = shifted(coeffs[:, :face], "axial", -1)
    send_shape = (stators, capacity + KEY_ROWS + QB * samples, GE)
    send, mapped = pl.pallas_call(
        functools.partial(gap_kernel, samples, stators, blocks, face, rotor_start),
        out_shape=(jax.ShapeDtypeStruct(send_shape, F32), jax.ShapeDtypeStruct((QB * samples, GE), F32)),
        name="gap_send",
    )(table, coeffs, mortar, peer, block)
    got = lax.all_to_all(send, "stator", split_axis=0, concat_axis=0, tiled=True)
    adjoint, rim_out, grad = pl.pallas_call(
        functools.partial(element_kernel, face, rotor_start),
        out_shape=(
            jax.ShapeDtypeStruct((samples, edges), F32),
            jax.ShapeDtypeStruct((samples, face), F32),
            jax.ShapeDtypeStruct((1, elements), F32),
        ),
        name="element",
    )(table, back, coeffs, rim, elem_edge, curl_map, jacobian, flux_fwd, density.reshape(1, elements))
    lower = shifted(rim_out, "axial", 1)
    adjoint = pl.pallas_call(
        functools.partial(join_kernel, samples, stators, blocks, face, rotor_start),
        out_shape=jax.ShapeDtypeStruct((samples, edges), F32),
        name="join",
    )(back, adjoint, lower, got, mapped, mortar, peer, block)
    return adjoint, grad.reshape(elements)


def solution(mesh):
    placed = (
        P(None, ("stator", "axial")),
        P(None, ("stator", "axial")),
        P(None, None, ("stator", "axial")),
        P(None, None, ("stator", "axial")),
        P(None, None, ("stator", "axial")),
        P(("stator", "axial")),
        P(),
        P(("stator", "axial"), None),
        P(("stator", "axial")),
    )
    return jax.shard_map(
        on_device,
        mesh=mesh,
        in_specs=placed,
        out_specs=(P(None, ("stator", "axial")), P(("stator", "axial"))),
        check_vma=False,
    )
```

```python
import functools
import math

import jax
import jax.numpy as jnp
import numpy as np
from jax import lax
from jax.experimental import pallas as pl
from jax.experimental.pallas import tpu as pltpu
from jax.sharding import PartitionSpec as P

GE = 128
QB = 2
LANES = 128
WIDE = 256
CHUNK = 256
LOOK = (1, 3, 5)
NEAR_BYTES = 1 << 20

PENALTY = 4.0
SIMP_POWER = 3.0

BF = jnp.bfloat16
F32 = jnp.float32


def shifted(value, axis, steps):
    count = lax.axis_size(axis)
    leading, last = (max(0, -steps), min(count, count - steps))
    return lax.ppermute(value, axis, [(source, source + steps) for source in range(leading, last)])


def dft_table(count):
    rows = np.arange(count, dtype=np.float64)[:, None]
    index = np.arange(count)
    harmonic = ((index + 1) // 2)[None, :]
    is_sine = ((index % 2 == 0) & (index > 0))[None, :]
    angle = 2.0 * math.pi * harmonic * rows / count
    return np.where(is_sine, np.sin(angle), np.cos(angle)) * math.sqrt(2.0 / count)


def table_parts(table):
    high = table.astype(BF)
    low = (table - high.astype(np.float64)).astype(BF)
    return np.concatenate([high, high, low, low], 1)


def split(value):
    high = value.astype(BF)
    low = (value - high.astype(F32)).astype(BF)
    return high, low


def dot(left, right):
    return jnp.dot(left, right, preferred_element_type=F32)


def dot_t(left, right):
    return lax.dot_general(left, right, (((1,), (1,)), ((), ())), preferred_element_type=F32)


def apply_table(table, value):
    high, low = split(value)
    return dot(table, jnp.concatenate([high, low, high, low], 0))


def iota(shape, dim):
    return lax.broadcasted_iota(jnp.int32, shape, dim)


def sorted_rows(peer_ref, block_ref, samples, blocks):
    rows = samples * blocks
    old, new = iota((rows, rows), 0), iota((rows, rows), 1)
    move = jnp.where(old == (new % samples) * blocks + new // samples, 1.0, 0.0).astype(BF)
    both = jnp.concatenate([peer_ref[...], block_ref[...]], 0).astype(F32)
    both = jnp.concatenate([both, jnp.zeros((6, rows), F32)], 0).astype(BF)
    moved = dot(both, move)
    return moved[0:1], moved[1:2]


def gap_kernel(
    samples, stators, blocks, face, rotor_start, table_ref, coeffs_ref, mortar_ref, peer_ref, block_ref,
    send_ref, turned_ref, rim_ref,
):
    rows = samples * blocks
    slots = 2 * rows
    capacity = slots // stators
    face_rows = QB * samples
    rim_ref[...] = coeffs_ref[:, :face]
    table = table_ref[...]
    face_time = apply_table(table, coeffs_ref[:, face : face + QB * GE])
    rotor_time = apply_table(table, coeffs_ref[:, rotor_start : rotor_start + blocks * GE])
    faces = jnp.concatenate([face_time[:, q * GE : (q + 1) * GE] for q in range(QB)], 0)
    rotors = jnp.concatenate([rotor_time[:, b * GE : (b + 1) * GE] for b in range(blocks)], 0)
    mortar_high, mortar_low = split(mortar_ref[...])
    mortar_down = jnp.concatenate([mortar_high, mortar_high, mortar_low], 0)
    mortar_across = jnp.concatenate([mortar_high, mortar_high, mortar_low], 1)

    def triple(value):
        high, low = split(value)
        return jnp.concatenate([high, low, high], 1)

    mapped = dot(triple(faces), mortar_down)
    turned_ref[...] = dot_t(triple(mapped), mortar_across)
    rotor_turned = dot_t(triple(rotors), mortar_across)
    peers, chosen = sorted_rows(peer_ref, block_ref, samples, blocks)
    across = jnp.broadcast_to(peers, (rows, rows))
    down = jnp.transpose(across)
    ahead = (across == down) & (iota((rows, rows), 0) < iota((rows, rows), 1))
    rank = jnp.sum(jnp.where(ahead, 1.0, 0.0), 0, keepdims=True)
    place = peers * capacity + rank
    slot = iota((slots, rows), 0).astype(F32)
    pick = jnp.where(slot == place, 1.0, 0.0).astype(BF)
    rotor_high, rotor_low = split(rotor_turned)
    picked = dot(pick, jnp.concatenate([rotor_high, rotor_low], 1))
    packed = picked[:, :GE] + picked[:, GE:]
    key = chosen * samples + (iota((1, rows), 1) % samples).astype(F32) + 1.0
    keys = dot_t(jnp.broadcast_to(key, (8, rows)).astype(BF), pick)
    for p in range(stators):
        first = p * (face_rows + capacity + 1)
        send_ref[first : first + face_rows, :] = mapped
        first += face_rows
        send_ref[first : first + capacity, :] = packed[p * capacity : (p + 1) * capacity]
        first += capacity
        start = p * capacity
        part = keys[:, start // LANES * LANES : (start // LANES + 1) * LANES]
        turn = (LANES - start % LANES) % LANES
        if turn:
            part = pltpu.roll(part, turn, 1)
        send_ref[first : first + 1, :] = part[:1]


def choose_kernel(samples, stators, blocks, wide_ref, peer_ref, block_ref, after_ref, out_ref):
    rows = samples * blocks
    pairs = stators * QB
    wanted = (peer_ref[...] * QB + block_ref[...]).astype(F32)
    wanted = jnp.broadcast_to(wanted, (8, rows)).astype(BF)
    lane = iota((rows, LANES), 1) % samples
    row = iota((rows, LANES), 0)
    spread = jnp.concatenate(
        [jnp.where(row == lane * blocks + b, 1.0, 0.0).astype(BF) for b in range(blocks)], 1
    )
    wanted = dot(wanted, spread)
    each = LANES // samples
    owner = (iota((samples, LANES), 1) // samples).astype(F32)
    for piece in range(2):
        values = wide_ref[piece * samples : (piece + 1) * samples, :].astype(F32)
        for b in range(blocks):
            want = jnp.broadcast_to(wanted[0:1, b * LANES : (b + 1) * LANES], (samples, LANES))
            for v in range(pairs // each):
                out_ref[(piece * blocks + b) * samples : (piece * blocks + b + 1) * samples,
                        v * LANES : (v + 1) * LANES] = jnp.where(want == owner + v * each, values, 0.0).astype(BF)


def element_kernel(
    face, rotor_start, table_ref, back_ref, coeffs_ref, rim_ref, edge_ref, curl_ref, jac_ref, fwd_ref, density_ref,
    adjoint_ref, rim_out_ref, grad_ref,
):
    samples, edges = coeffs_ref.shape
    elements = edge_ref.shape[1]
    table = table_ref[...]
    own_time = apply_table(table, coeffs_ref[...])
    rim_time = apply_table(table, rim_ref[:, :face])
    total = edges + face
    wides = -(-total // WIDE)
    whole = jnp.concatenate([own_time, rim_time], 1)
    extended = [whole[:, i * LANES : (i + 1) * LANES] for i in range(total // LANES)]
    padded = jnp.concatenate([whole, jnp.zeros((samples, wides * WIDE - total), F32)], 1)
    stack = jnp.concatenate(
        [part for w in range(wides) for part in split(padded[:, w * WIDE : (w + 1) * WIDE])], 0
    )
    places = iota((WIDE, LANES), 0).astype(F32).astype(BF)
    summed = jnp.zeros((wides * 2 * samples, WIDE), F32)
    for chunk in range(elements // CHUNK):
        lane_slices = [
            slice(chunk * CHUNK + half * LANES, chunk * CHUNK + (half + 1) * LANES) for half in range(CHUNK // LANES)
        ]
        rights = []
        for m in range(6):
            parts = []
            for lanes in lane_slices:
                index = edge_ref[m : m + 1, lanes]
                place = jnp.broadcast_to(index & (WIDE - 1), (16, LANES)).astype(F32).astype(BF)
                place = jnp.concatenate([place] * (WIDE // 16), 0)
                parts.append(jnp.where(place == places, jnp.ones_like(place), jnp.zeros_like(place)))
            rights.append(jnp.concatenate(parts, 1))
        looked = {m: dot(stack, rights[m]) for m in LOOK}
        left_lanes = [[] for _ in range(6)]
        for half, lanes in enumerate(lane_slices):
            at = slice(half * LANES, (half + 1) * LANES)
            values = []
            for m in range(6):
                index = edge_ref[m : m + 1, lanes]
                if m in LOOK:
                    found = [
                        looked[m][2 * w * samples : (2 * w + 1) * samples, at]
                        + looked[m][(2 * w + 1) * samples : (2 * w + 2) * samples, at]
                        for w in range(wides)
                    ]
                    high = jnp.broadcast_to(index // WIDE, (samples, LANES))
                else:
                    low = jnp.broadcast_to(index & (LANES - 1), (samples, LANES))
                    found = [
                        jnp.take_along_axis(part, low, axis=1, mode="promise_in_bounds") for part in extended
                    ]
                    high = jnp.broadcast_to(index // LANES, (samples, LANES))
                bit = 1
                while len(found) > 1:
                    odd = (high & bit) != 0
                    found = [
                        jnp.where(odd, found[i + 1], found[i]) if i + 1 < len(found) else found[i]
                        for i in range(0, len(found), 2)
                    ]
                    bit *= 2
                values.append(found[0])
            curl = [[curl_ref[c, m : m + 1, lanes] for m in range(6)] for c in range(3)]
            flux = []
            for c in range(3):
                acc = curl[c][0] * values[0]
                for m in range(1, 6):
                    acc = acc + curl[c][m] * values[m]
                flux.append(acc)
            energy = flux[0] * fwd_ref[0, :, lanes].astype(F32)
            for c in range(1, 3):
                energy = energy + flux[c] * fwd_ref[c, :, lanes].astype(F32)
            energy = jnp.sum(energy, 0, keepdims=True)
            density = density_ref[:, lanes]
            grad_ref[:, lanes] = SIMP_POWER * density * density * energy / samples
            jac = [jac_ref[k, :, lanes].astype(F32) for k in range(6)]
            field = [
                jac[0] * flux[0] + jac[3] * flux[1] + jac[4] * flux[2],
                jac[3] * flux[0] + jac[1] * flux[1] + jac[5] * flux[2],
                jac[4] * flux[0] + jac[5] * flux[1] + jac[2] * flux[2],
            ]
            for m in range(6):
                term = curl[0][m] * field[0] + curl[1][m] * field[1] + curl[2][m] * field[2]
                high, low = split(term)
                pair = jnp.concatenate([high, low], 0)
                index = edge_ref[m : m + 1, lanes]
                wide = jnp.broadcast_to(index // WIDE, (16, LANES)).astype(F32).astype(BF)
                wide = jnp.concatenate([wide] * (2 * samples // 16), 0)
                left_lanes[m].append(
                    jnp.concatenate([jnp.where(wide == w, pair, jnp.zeros_like(pair)) for w in range(wides)], 0)
                )
        left = jnp.concatenate([part for m in range(6) for part in left_lanes[m]], 1)
        summed = summed + dot_t(left, jnp.concatenate(rights, 1))
    pieces = []
    for w in range(wides):
        base = w * 2 * samples
        pieces.append(summed[base : base + samples] + summed[base + samples : base + 2 * samples])
    residual = jnp.concatenate(pieces, 1)
    own = jnp.concatenate(
        [residual[:, :rotor_start], residual[:, rotor_start:edges] + PENALTY * own_time[:, rotor_start:]], 1
    )
    back = back_ref[...]
    adjoint_ref[...] = apply_table(back, own)
    rim_out_ref[...] = apply_table(back, residual[:, edges:total])


def join_kernel(
    samples, stators, blocks, face, rotor_start, back_ref, adjoint_ref, rim_ref, got_ref, turned_ref, choose_ref,
    out_ref,
):
    slots = 2 * samples * blocks
    capacity = slots // stators
    face_rows = QB * samples
    keys_at = face_rows + capacity
    each = keys_at + 1
    faces = jnp.concatenate([got_ref[p * each : p * each + face_rows, :] for p in range(stators)], 0)
    face_high, face_low = split(faces)
    facing = dot(choose_ref[...], jnp.concatenate([face_high, face_low], 1))
    rows = blocks * samples
    facing = (facing[:rows, :GE] + facing[:rows, GE:]) + (facing[rows:, :GE] + facing[rows:, GE:])

    lane = iota((1, LANES), 1)
    key_parts = []
    for v in range(slots // LANES):
        acc = jnp.zeros((1, LANES), F32)
        for p in range(v * LANES // capacity, (v + 1) * LANES // capacity):
            part = jnp.where(lane < capacity, got_ref[p * each + keys_at : (p + 1) * each, :], 0.0)
            turn = p * capacity % LANES
            acc = acc + (pltpu.roll(part, turn, 1) if turn else part)
        key_parts.append(acc[0:1])
    key = jnp.concatenate(key_parts, 1)
    hit = jnp.where(key == (iota((face_rows, slots), 0) + 1).astype(F32), 1.0, 0.0)
    count = jnp.sum(hit, 1, keepdims=True)
    packed = jnp.concatenate([got_ref[p * each + face_rows : p * each + keys_at, :] for p in range(stators)], 0)
    packed_high, packed_low = split(packed)
    gathered = dot(hit.astype(BF), jnp.concatenate([packed_high, packed_low], 1))
    gathered = (gathered[:, :GE] + gathered[:, GE:] - count * turned_ref[...]) * (-PENALTY)
    stator_term = jnp.concatenate([gathered[q * samples : (q + 1) * samples] for q in range(QB)], 1)
    stator_term = apply_table(back_ref[...], stator_term)
    out_ref[:, :face] = adjoint_ref[:, :face] + rim_ref[...]
    out_ref[:, face : face + QB * GE] = adjoint_ref[:, face : face + QB * GE] + stator_term
    out_ref[:, face + QB * GE : rotor_start] = adjoint_ref[:, face + QB * GE : rotor_start]
    for b in range(blocks):
        at = slice(rotor_start + b * GE, rotor_start + (b + 1) * GE)
        out_ref[:, at] = adjoint_ref[:, at] + facing[b * samples : (b + 1) * samples]


def small(shape, kind):
    return math.prod(shape) * jnp.dtype(kind).itemsize <= NEAR_BYTES


def call(kernel, near, *shapes):
    spec = lambda inside: pl.BlockSpec(memory_space=pltpu.VMEM) if inside else pl.BlockSpec()

    def run(*operands):
        close = [near and small(operand.shape, operand.dtype) for operand in operands]
        operands = [
            pltpu.with_memory_space_constraint(operand, pltpu.VMEM) if inside else operand
            for inside, operand in zip(close, operands)
        ]
        return pl.pallas_call(
            kernel,
            out_shape=[
                pltpu.VMEM(shape, kind) if inside and small(shape, kind) else jax.ShapeDtypeStruct(shape, kind)
                for inside, shape, kind in shapes
            ],
            in_specs=[spec(inside) for inside in close],
            out_specs=[spec(inside and small(shape, kind)) for inside, shape, kind in shapes],
        )(*operands)

    return run


def on_device(coeffs, elem_edge, curl_map, jacobian, flux_fwd, density, mortar, gap_peer, gap_block):
    stators = lax.axis_size("stator")
    samples, edges = coeffs.shape
    rows = gap_block.shape[0]
    blocks = rows // samples
    capacity = 2 * rows // stators
    face = edges // 8
    rotor_start = edges - blocks * GE
    elements = density.shape[0]
    face_rows = QB * samples
    table_value = dft_table(samples)
    table = jnp.asarray(table_parts(table_value))
    back = jnp.asarray(table_parts(table_value.T))
    wide = -PENALTY * table_value.T
    wide_high = wide.astype(BF)
    wide_low = (wide - wide_high.astype(np.float64)).astype(BF)
    wide = jnp.asarray(np.tile(np.concatenate([wide_high, wide_low], 0), (1, LANES // samples)))
    peer = gap_peer.reshape(1, rows)
    block = gap_block.reshape(1, rows)
    send, turned, rim = call(
        functools.partial(gap_kernel, samples, stators, blocks, face, rotor_start),
        False,
        (False, (stators * (face_rows + capacity + 1), GE), F32),
        (True, (face_rows, GE), F32),
        (True, (samples, face), F32),
    )(table, coeffs, mortar, peer, block)
    rim = shifted(rim, "axial", -1)
    parts = send.reshape(stators, face_rows + capacity + 1, 1, GE)
    got = lax.all_to_all(parts, "stator", split_axis=0, concat_axis=0, tiled=True).reshape(send.shape)
    adjoint, rim_out, grad = call(
        functools.partial(element_kernel, face, rotor_start),
        True,
        (True, (samples, edges), F32),
        (True, (samples, face), F32),
        (False, (1, elements), F32),
    )(table, back, coeffs, rim, elem_edge, curl_map, jacobian, flux_fwd, density.reshape(1, elements))
    lower = shifted(rim_out, "axial", 1)
    (choose,) = call(
        functools.partial(choose_kernel, samples, stators, blocks), True, (True, (2 * rows, stators * face_rows), BF)
    )(wide, peer, block, rim_out)
    (adjoint,) = call(
        functools.partial(join_kernel, samples, stators, blocks, face, rotor_start),
        True,
        (False, (samples, edges), F32),
    )(back, adjoint, lower, got, turned, choose)
    return adjoint, grad.reshape(elements)


def solution(mesh):
    placed = (
        P(None, ("stator", "axial")),
        P(None, ("stator", "axial")),
        P(None, None, ("stator", "axial")),
        P(None, None, ("stator", "axial")),
        P(None, None, ("stator", "axial")),
        P(("stator", "axial")),
        P(),
        P(("stator", "axial"), None),
        P(("stator", "axial")),
    )
    return jax.shard_map(
        on_device,
        mesh=mesh,
        in_specs=placed,
        out_specs=(P(None, ("stator", "axial")), P(("stator", "axial"))),
        check_vma=False,
    )
```

```python
import functools
import math

import jax
import jax.numpy as jnp
import numpy as np
from jax import lax
from jax.experimental import pallas as pl
from jax.experimental.pallas import tpu as pltpu
from jax.sharding import PartitionSpec as P

GE = 128
QB = 2
LANES = 128
WIDE = 256
CHUNK = 256
LOOK = (1, 3, 5)
NEAR_BYTES = 1 << 20

PENALTY = 4.0
SIMP_POWER = 3.0

BF = jnp.bfloat16
F32 = jnp.float32


def shifted(value, axis, steps):
    count = lax.axis_size(axis)
    leading, last = (max(0, -steps), min(count, count - steps))
    return lax.ppermute(value, axis, [(source, source + steps) for source in range(leading, last)])


def dft_table(count):
    rows = np.arange(count, dtype=np.float64)[:, None]
    index = np.arange(count)
    harmonic = ((index + 1) // 2)[None, :]
    is_sine = ((index % 2 == 0) & (index > 0))[None, :]
    angle = 2.0 * math.pi * harmonic * rows / count
    return np.where(is_sine, np.sin(angle), np.cos(angle)) * math.sqrt(2.0 / count)


def table_parts(table):
    high = table.astype(BF)
    low = (table - high.astype(np.float64)).astype(BF)
    return np.concatenate([high, high, low, low], 1)


def split(value):
    high = value.astype(BF)
    low = (value - high.astype(F32)).astype(BF)
    return high, low


def dot(left, right):
    return jnp.dot(left, right, preferred_element_type=F32)


def dot_t(left, right):
    return lax.dot_general(left, right, (((1,), (1,)), ((), ())), preferred_element_type=F32)


def apply_table(table, value):
    high, low = split(value)
    return dot(table, jnp.concatenate([high, low, high, low], 0))


def iota(shape, dim):
    return lax.broadcasted_iota(jnp.int32, shape, dim)


def triple(value):
    high, low = split(value)
    return jnp.concatenate([high, low, high], 1)


def gap_kernel(
    samples, stators, blocks, face, rotor_start, table_far, coeffs_far, mortar_far, peer_far, block_far,
    send_ref, mapped_ref, rim_ref, table_ref, coeffs_ref, mortar_ref, peer_ref, block_ref, sems,
):
    fars = (peer_far, block_far, coeffs_far, table_far, mortar_far)
    nears = (peer_ref, block_ref, coeffs_ref, table_ref, mortar_ref)
    copies = [pltpu.make_async_copy(far, near, sems.at[i]) for i, (far, near) in enumerate(zip(fars, nears))]
    for copy in copies:
        copy.start()
    rows = samples * blocks
    slots = 2 * rows
    capacity = slots // stators
    face_rows = QB * samples
    old, new = iota((rows, rows), 0), iota((rows, rows), 1)
    move = jnp.where(old == (new % samples) * blocks + new // samples, 1.0, 0.0).astype(BF)
    earlier = jnp.where(old < new, 1.0, 0.0)
    slot = iota((slots, rows), 0).astype(F32)
    sample = (iota((1, rows), 1) % samples).astype(F32) + 1.0
    for copy in copies:
        copy.wait()
    both = jnp.concatenate([peer_ref[...], block_ref[...]], 0).astype(F32)
    both = jnp.concatenate([both, jnp.zeros((6, rows), F32)], 0).astype(BF)
    both = dot(both, move)
    peers, chosen = both[0:1], both[1:2]
    rim_ref[...] = coeffs_ref[:, :face]
    table = table_ref[...]
    rotor_time = apply_table(table, coeffs_ref[:, rotor_start : rotor_start + blocks * GE])
    face_time = apply_table(table, coeffs_ref[:, face : face + QB * GE])
    rotors = jnp.concatenate([rotor_time[:, b * GE : (b + 1) * GE] for b in range(blocks)], 0)
    faces = jnp.concatenate([face_time[:, q * GE : (q + 1) * GE] for q in range(QB)], 0)
    mortar_high, mortar_low = split(mortar_ref[...])
    mortar_down = jnp.concatenate([mortar_high, mortar_high, mortar_low], 0)
    mortar_across = jnp.concatenate([mortar_high, mortar_high, mortar_low], 1)
    rotor_turned = dot_t(triple(rotors), mortar_across)
    mapped = dot(triple(faces), mortar_down)
    mapped_ref[...] = mapped
    across = jnp.broadcast_to(peers, (rows, rows))
    down = jnp.transpose(across)
    rank = jnp.sum(jnp.where(across == down, earlier, 0.0), 0, keepdims=True)
    place = peers * capacity + rank
    pick = jnp.where(slot == place, 1.0, 0.0).astype(BF)
    rotor_high, rotor_low = split(rotor_turned)
    picked = dot(pick, jnp.concatenate([rotor_high, rotor_low], 1))
    packed = picked[:, :GE] + picked[:, GE:]
    key = chosen * samples + sample
    keys = dot_t(jnp.broadcast_to(key, (8, rows)).astype(BF), pick)
    for p in range(stators):
        first = p * (face_rows + capacity + 1)
        send_ref[first : first + face_rows, :] = mapped
        first += face_rows
        send_ref[first : first + capacity, :] = packed[p * capacity : (p + 1) * capacity]
        first += capacity
        start = p * capacity
        part = keys[:, start // LANES * LANES : (start // LANES + 1) * LANES]
        turn = (LANES - start % LANES) % LANES
        if turn:
            part = pltpu.roll(part, turn, 1)
        send_ref[first : first + 1, :] = part[:1]


def choose_kernel(
    samples, stators, blocks, wide_ref, peer_ref, block_ref, mapped_ref, mortar_ref, after_ref, out_ref, turned_ref
):
    mortar_high, mortar_low = split(mortar_ref[...])
    mortar_across = jnp.concatenate([mortar_high, mortar_high, mortar_low], 1)
    turned_ref[...] = dot_t(triple(mapped_ref[...]), mortar_across)
    rows = samples * blocks
    pairs = stators * QB
    wanted = (peer_ref[...] * QB + block_ref[...]).astype(F32)
    wanted = jnp.broadcast_to(wanted, (8, rows)).astype(BF)
    lane = iota((rows, LANES), 1) % samples
    row = iota((rows, LANES), 0)
    spread = jnp.concatenate(
        [jnp.where(row == lane * blocks + b, 1.0, 0.0).astype(BF) for b in range(blocks)], 1
    )
    wanted = dot(wanted, spread)
    each = LANES // samples
    owner = (iota((samples, LANES), 1) // samples).astype(F32)
    for piece in range(2):
        values = wide_ref[piece * samples : (piece + 1) * samples, :].astype(F32)
        for b in range(blocks):
            want = jnp.broadcast_to(wanted[0:1, b * LANES : (b + 1) * LANES], (samples, LANES))
            for v in range(pairs // each):
                out_ref[(piece * blocks + b) * samples : (piece * blocks + b + 1) * samples,
                        v * LANES : (v + 1) * LANES] = jnp.where(want == owner + v * each, values, 0.0).astype(BF)


def element_kernel(
    face, rotor_start, table_ref, back_ref, coeffs_ref, rim_ref, edge_ref, curl_ref, jac_ref, fwd_ref, density_ref,
    adjoint_ref, rim_out_ref, grad_ref,
):
    samples, edges = coeffs_ref.shape
    elements = edge_ref.shape[1]
    table = table_ref[...]
    own_time = apply_table(table, coeffs_ref[...])
    rim_time = apply_table(table, rim_ref[:, :face])
    total = edges + face
    wides = -(-total // WIDE)
    whole = jnp.concatenate([own_time, rim_time], 1)
    extended = [whole[:, i * LANES : (i + 1) * LANES] for i in range(total // LANES)]
    padded = jnp.concatenate([whole, jnp.zeros((samples, wides * WIDE - total), F32)], 1)
    stack = jnp.concatenate(
        [part for w in range(wides) for part in split(padded[:, w * WIDE : (w + 1) * WIDE])], 0
    )
    places = iota((WIDE, LANES), 0).astype(F32).astype(BF)
    summed = jnp.zeros((wides * 2 * samples, WIDE), F32)
    for chunk in range(elements // CHUNK):
        lane_slices = [
            slice(chunk * CHUNK + half * LANES, chunk * CHUNK + (half + 1) * LANES) for half in range(CHUNK // LANES)
        ]
        rights = []
        for m in range(6):
            parts = []
            for lanes in lane_slices:
                index = edge_ref[m : m + 1, lanes]
                place = jnp.broadcast_to(index & (WIDE - 1), (16, LANES)).astype(F32).astype(BF)
                place = jnp.concatenate([place] * (WIDE // 16), 0)
                parts.append(jnp.where(place == places, jnp.ones_like(place), jnp.zeros_like(place)))
            rights.append(jnp.concatenate(parts, 1))
        looked = {m: dot(stack, rights[m]) for m in LOOK}
        left_lanes = [[] for _ in range(6)]
        for half, lanes in enumerate(lane_slices):
            at = slice(half * LANES, (half + 1) * LANES)
            values = []
            for m in range(6):
                index = edge_ref[m : m + 1, lanes]
                if m in LOOK:
                    found = [
                        looked[m][2 * w * samples : (2 * w + 1) * samples, at]
                        + looked[m][(2 * w + 1) * samples : (2 * w + 2) * samples, at]
                        for w in range(wides)
                    ]
                    high = jnp.broadcast_to(index // WIDE, (samples, LANES))
                else:
                    low = jnp.broadcast_to(index & (LANES - 1), (samples, LANES))
                    found = [
                        jnp.take_along_axis(part, low, axis=1, mode="promise_in_bounds") for part in extended
                    ]
                    high = jnp.broadcast_to(index // LANES, (samples, LANES))
                bit = 1
                while len(found) > 1:
                    odd = (high & bit) != 0
                    found = [
                        jnp.where(odd, found[i + 1], found[i]) if i + 1 < len(found) else found[i]
                        for i in range(0, len(found), 2)
                    ]
                    bit *= 2
                values.append(found[0])
            curl = [[curl_ref[c, m : m + 1, lanes] for m in range(6)] for c in range(3)]
            flux = []
            for c in range(3):
                acc = curl[c][0] * values[0]
                for m in range(1, 6):
                    acc = acc + curl[c][m] * values[m]
                flux.append(acc)
            energy = flux[0] * fwd_ref[0, :, lanes].astype(F32)
            for c in range(1, 3):
                energy = energy + flux[c] * fwd_ref[c, :, lanes].astype(F32)
            energy = jnp.sum(energy, 0, keepdims=True)
            density = density_ref[:, lanes]
            grad_ref[:, lanes] = SIMP_POWER * density * density * energy / samples
            jac = [jac_ref[k, :, lanes].astype(F32) for k in range(6)]
            field = [
                jac[0] * flux[0] + jac[3] * flux[1] + jac[4] * flux[2],
                jac[3] * flux[0] + jac[1] * flux[1] + jac[5] * flux[2],
                jac[4] * flux[0] + jac[5] * flux[1] + jac[2] * flux[2],
            ]
            for m in range(6):
                term = curl[0][m] * field[0] + curl[1][m] * field[1] + curl[2][m] * field[2]
                high, low = split(term)
                pair = jnp.concatenate([high, low], 0)
                index = edge_ref[m : m + 1, lanes]
                wide = jnp.broadcast_to(index // WIDE, (16, LANES)).astype(F32).astype(BF)
                wide = jnp.concatenate([wide] * (2 * samples // 16), 0)
                left_lanes[m].append(
                    jnp.concatenate([jnp.where(wide == w, pair, jnp.zeros_like(pair)) for w in range(wides)], 0)
                )
        left = jnp.concatenate([part for m in range(6) for part in left_lanes[m]], 1)
        summed = summed + dot_t(left, jnp.concatenate(rights, 1))
    pieces = []
    for w in range(wides):
        base = w * 2 * samples
        pieces.append(summed[base : base + samples] + summed[base + samples : base + 2 * samples])
    residual = jnp.concatenate(pieces, 1)
    own = jnp.concatenate(
        [residual[:, :rotor_start], residual[:, rotor_start:edges] + PENALTY * own_time[:, rotor_start:]], 1
    )
    back = back_ref[...]
    adjoint_ref[...] = apply_table(back, own)
    rim_out_ref[...] = apply_table(back, residual[:, edges:total])


def join_kernel(
    samples, stators, blocks, face, rotor_start, back_ref, adjoint_ref, rim_ref, got_ref, turned_ref, choose_ref,
    out_ref,
):
    slots = 2 * samples * blocks
    capacity = slots // stators
    face_rows = QB * samples
    keys_at = face_rows + capacity
    each = keys_at + 1
    faces = jnp.concatenate([got_ref[p * each : p * each + face_rows, :] for p in range(stators)], 0)
    face_high, face_low = split(faces)
    facing = dot(choose_ref[...], jnp.concatenate([face_high, face_low], 1))
    rows = blocks * samples
    facing = (facing[:rows, :GE] + facing[:rows, GE:]) + (facing[rows:, :GE] + facing[rows:, GE:])

    lane = iota((1, LANES), 1)
    key_parts = []
    for v in range(slots // LANES):
        acc = jnp.zeros((1, LANES), F32)
        for p in range(v * LANES // capacity, (v + 1) * LANES // capacity):
            part = jnp.where(lane < capacity, got_ref[p * each + keys_at : (p + 1) * each, :], 0.0)
            turn = p * capacity % LANES
            acc = acc + (pltpu.roll(part, turn, 1) if turn else part)
        key_parts.append(acc[0:1])
    key = jnp.concatenate(key_parts, 1)
    hit = jnp.where(key == (iota((face_rows, slots), 0) + 1).astype(F32), 1.0, 0.0)
    count = jnp.sum(hit, 1, keepdims=True)
    packed = jnp.concatenate([got_ref[p * each + face_rows : p * each + keys_at, :] for p in range(stators)], 0)
    packed_high, packed_low = split(packed)
    gathered = dot(hit.astype(BF), jnp.concatenate([packed_high, packed_low], 1))
    gathered = (gathered[:, :GE] + gathered[:, GE:] - count * turned_ref[...]) * (-PENALTY)
    stator_term = jnp.concatenate([gathered[q * samples : (q + 1) * samples] for q in range(QB)], 1)
    stator_term = apply_table(back_ref[...], stator_term)
    out_ref[:, :face] = adjoint_ref[:, :face] + rim_ref[...]
    out_ref[:, face : face + QB * GE] = adjoint_ref[:, face : face + QB * GE] + stator_term
    out_ref[:, face + QB * GE : rotor_start] = adjoint_ref[:, face + QB * GE : rotor_start]
    for b in range(blocks):
        at = slice(rotor_start + b * GE, rotor_start + (b + 1) * GE)
        out_ref[:, at] = adjoint_ref[:, at] + facing[b * samples : (b + 1) * samples]


def small(shape, kind):
    return math.prod(shape) * jnp.dtype(kind).itemsize <= NEAR_BYTES


def call(kernel, near, *shapes, far=(), scratch=()):
    def spec(inside, anywhere=False):
        if anywhere:
            return pl.BlockSpec(memory_space=pl.ANY)
        return pl.BlockSpec(memory_space=pltpu.VMEM) if inside else pl.BlockSpec()

    def run(*operands):
        close = [near and small(operand.shape, operand.dtype) for operand in operands]
        operands = [
            pltpu.with_memory_space_constraint(operand, pltpu.VMEM) if inside else operand
            for inside, operand in zip(close, operands)
        ]
        return pl.pallas_call(
            kernel,
            out_shape=[
                pltpu.VMEM(shape, kind) if inside and small(shape, kind) else jax.ShapeDtypeStruct(shape, kind)
                for inside, shape, kind in shapes
            ],
            in_specs=[spec(inside) for inside in close] + [spec(False, True)] * len(far),
            out_specs=[spec(inside and small(shape, kind)) for inside, shape, kind in shapes],
            scratch_shapes=scratch,
        )(*operands, *far)

    return run


def on_device(coeffs, elem_edge, curl_map, jacobian, flux_fwd, density, mortar, gap_peer, gap_block):
    stators = lax.axis_size("stator")
    samples, edges = coeffs.shape
    rows = gap_block.shape[0]
    blocks = rows // samples
    capacity = 2 * rows // stators
    face = edges // 8
    rotor_start = edges - blocks * GE
    elements = density.shape[0]
    face_rows = QB * samples
    table_value = dft_table(samples)
    table = jnp.asarray(table_parts(table_value))
    back = jnp.asarray(table_parts(table_value.T))
    wide = -PENALTY * table_value.T
    wide_high = wide.astype(BF)
    wide_low = (wide - wide_high.astype(np.float64)).astype(BF)
    wide = jnp.asarray(np.tile(np.concatenate([wide_high, wide_low], 0), (1, LANES // samples)))
    peer = gap_peer.reshape(1, rows)
    block = gap_block.reshape(1, rows)
    ahead = (table, coeffs, mortar, peer, block)
    send, mapped, rim = call(
        functools.partial(gap_kernel, samples, stators, blocks, face, rotor_start),
        False,
        (False, (stators * (face_rows + capacity + 1), GE), F32),
        (True, (face_rows, GE), F32),
        (True, (samples, face), F32),
        far=ahead,
        scratch=[pltpu.VMEM(value.shape, value.dtype) for value in ahead]
        + [pltpu.SemaphoreType.DMA((len(ahead),))],
    )()
    rim = shifted(rim, "axial", -1)
    parts = send.reshape(stators, face_rows + capacity + 1, 1, GE)
    got = lax.all_to_all(parts, "stator", split_axis=0, concat_axis=0, tiled=True).reshape(send.shape)
    adjoint, rim_out, grad = call(
        functools.partial(element_kernel, face, rotor_start),
        True,
        (True, (samples, edges), F32),
        (True, (samples, face), F32),
        (False, (1, elements), F32),
    )(table, back, coeffs, rim, elem_edge, curl_map, jacobian, flux_fwd, density.reshape(1, elements))
    lower = shifted(rim_out, "axial", 1)
    choose, turned = call(
        functools.partial(choose_kernel, samples, stators, blocks),
        True,
        (True, (2 * rows, stators * face_rows), BF),
        (True, (face_rows, GE), F32),
    )(wide, peer, block, mapped, mortar, rim_out)
    (adjoint,) = call(
        functools.partial(join_kernel, samples, stators, blocks, face, rotor_start),
        True,
        (False, (samples, edges), F32),
    )(back, adjoint, lower, got, turned, choose)
    return adjoint, grad.reshape(elements)


def solution(mesh):
    placed = (
        P(None, ("stator", "axial")),
        P(None, ("stator", "axial")),
        P(None, None, ("stator", "axial")),
        P(None, None, ("stator", "axial")),
        P(None, None, ("stator", "axial")),
        P(("stator", "axial")),
        P(),
        P(("stator", "axial"), None),
        P(("stator", "axial")),
    )
    return jax.shard_map(
        on_device,
        mesh=mesh,
        in_specs=placed,
        out_specs=(P(None, ("stator", "axial")), P(("stator", "axial"))),
        check_vma=False,
    )
```

```python
import functools
import math

import jax
import jax.numpy as jnp
import numpy as np
from jax import lax
from jax.experimental import pallas as pl
from jax.experimental.pallas import tpu as pltpu
from jax.sharding import PartitionSpec as P

GE = 128
QB = 2
LANES = 128
WIDE = 256
CHUNK = 256
LOOK = (1, 3, 5)
NEAR_BYTES = 1 << 20
MOST_PERMUTES = 8


PENALTY = 4.0
SIMP_POWER = 3.0

BF = jnp.bfloat16
F32 = jnp.float32


def shifted(value, axis, steps):
    count = lax.axis_size(axis)
    leading, last = (max(0, -steps), min(count, count - steps))
    return lax.ppermute(value, axis, [(source, source + steps) for source in range(leading, last)])


def dft_table(count):
    rows = np.arange(count, dtype=np.float64)[:, None]
    index = np.arange(count)
    harmonic = ((index + 1) // 2)[None, :]
    is_sine = ((index % 2 == 0) & (index > 0))[None, :]
    angle = 2.0 * math.pi * harmonic * rows / count
    return np.where(is_sine, np.sin(angle), np.cos(angle)) * math.sqrt(2.0 / count)


def table_parts(table):
    high = table.astype(BF)
    low = (table - high.astype(np.float64)).astype(BF)
    return np.concatenate([high, high, low, low], 1)


def split(value):
    high = value.astype(BF)
    low = (value - high.astype(F32)).astype(BF)
    return high, low


def dot(left, right):
    return jnp.dot(left, right, preferred_element_type=F32)


def dot_t(left, right):
    return lax.dot_general(left, right, (((1,), (1,)), ((), ())), preferred_element_type=F32)


def apply_table(table, value):
    high, low = split(value)
    return dot(table, jnp.concatenate([high, low, high, low], 0))


def iota(shape, dim):
    return lax.broadcasted_iota(jnp.int32, shape, dim)


def by_permutes(stators):
    return 4 <= stators <= MOST_PERMUTES and stators & (stators - 1) == 0


def places_of(peer_ref, stators):
    peers = peer_ref[...]
    return peers ^ lax.axis_index("stator") if by_permutes(stators) else peers


def triple(value):
    high, low = split(value)
    return jnp.concatenate([high, low, high], 1)


def gap_kernel(
    samples, stators, blocks, face, rotor_start, later, table_far, coeffs_far, mortar_far, peer_far, block_far, *refs,
):
    later_far, (mapped_ref, rim_ref), refs = refs[:later], refs[later : later + 2], refs[later + 2 :]
    later_near, refs = refs[:later], refs[later:]
    *send_refs, table_ref, coeffs_ref, mortar_ref, peer_ref, block_ref, sems, later_sems = refs
    fars = (peer_far, block_far, coeffs_far, table_far, mortar_far)
    nears = (peer_ref, block_ref, coeffs_ref, table_ref, mortar_ref)
    copies = [pltpu.make_async_copy(far, near, sems.at[i]) for i, (far, near) in enumerate(zip(fars, nears))]
    ahead = [pltpu.make_async_copy(far, near, later_sems.at[i]) for i, (far, near) in enumerate(zip(later_far, later_near))]
    for copy in copies + ahead:
        copy.start()
    rows = samples * blocks
    slots = 2 * rows
    capacity = slots // stators
    face_rows = QB * samples
    old, new = iota((rows, rows), 0), iota((rows, rows), 1)
    move = jnp.where(old == (new % samples) * blocks + new // samples, 1.0, 0.0).astype(BF)
    earlier = jnp.where(old < new, 1.0, 0.0)
    slot = iota((slots, rows), 0).astype(F32)
    sample = (iota((1, rows), 1) % samples).astype(F32) + 1.0
    for copy in copies:
        copy.wait()
    both = jnp.concatenate([places_of(peer_ref, stators), block_ref[...]], 0).astype(F32)
    both = jnp.concatenate([both, jnp.zeros((6, rows), F32)], 0).astype(BF)
    both = dot(both, move)
    peers, chosen = both[0:1], both[1:2]
    rim_ref[...] = coeffs_ref[:, :face]
    table = table_ref[...]
    rotor_time = apply_table(table, coeffs_ref[:, rotor_start : rotor_start + blocks * GE])
    face_time = apply_table(table, coeffs_ref[:, face : face + QB * GE])
    rotors = jnp.concatenate([rotor_time[:, b * GE : (b + 1) * GE] for b in range(blocks)], 0)
    faces = jnp.concatenate([face_time[:, q * GE : (q + 1) * GE] for q in range(QB)], 0)
    mortar_high, mortar_low = split(mortar_ref[...])
    mortar_down = jnp.concatenate([mortar_high, mortar_high, mortar_low], 0)
    mortar_across = jnp.concatenate([mortar_high, mortar_high, mortar_low], 1)
    rotor_turned = dot_t(triple(rotors), mortar_across)
    mapped = dot(triple(faces), mortar_down)
    mapped_ref[...] = mapped
    across = jnp.broadcast_to(peers, (rows, rows))
    down = jnp.transpose(across)
    rank = jnp.sum(jnp.where(across == down, earlier, 0.0), 0, keepdims=True)
    place = peers * capacity + rank
    pick = jnp.where(slot == place, 1.0, 0.0).astype(BF)
    rotor_high, rotor_low = split(rotor_turned)
    picked = dot(pick, jnp.concatenate([rotor_high, rotor_low], 1))
    packed = picked[:, :GE] + picked[:, GE:]
    key = chosen * samples + sample
    keys = dot_t(jnp.broadcast_to(key, (8, rows)).astype(BF), pick)
    spots = send_spots(stators, face_rows, capacity)
    for p in range(stators):
        start = p * capacity
        part = keys[:, start // LANES * LANES : (start // LANES + 1) * LANES]
        turn = (LANES - start % LANES) % LANES
        if turn:
            part = pltpu.roll(part, turn, 1)
        which, face_at, slot_at, key_at = spots[p]
        if face_at is not None:
            send_refs[which][face_at : face_at + face_rows, :] = mapped
        send_refs[which][slot_at : slot_at + capacity, :] = packed[start : start + capacity]
        send_refs[which][key_at : key_at + 1, :] = part[:1]
    for copy in ahead:
        copy.wait()


def send_spots(stators, face_rows, capacity):
    each = face_rows + capacity + 1
    if not by_permutes(stators):
        return [(0, p * each, p * each + face_rows, (p + 1) * each - 1) for p in range(stators)]
    spots = [(0, 0, face_rows, each - 1), (1, 0, face_rows, each - 1)]
    for p in range(2, stators, 2):
        last = face_rows + 2 * capacity
        spots.append((1 + p // 2, 0, face_rows, last))
        spots.append((1 + p // 2, None, face_rows + capacity, last + 1))
    return spots


def got_spots(stators, face_rows, capacity):
    each = face_rows + capacity + 1
    spots = send_spots(stators, face_rows, capacity)
    if by_permutes(stators):
        for p in range(3, stators, 2):
            base = (p - 3) // 2 * each
            spots[p] = (1 + stators // 2, base, base + face_rows, base + each - 1)
    return spots


def relay_kernel(face_rows, capacity, *refs):
    *got_refs, after_ref, out_ref = refs
    each = face_rows + capacity + 1
    last = face_rows + 2 * capacity + 1
    for i, got_ref in enumerate(got_refs):
        base = i * each
        out_ref[base : base + face_rows, :] = got_ref[:face_rows, :]
        out_ref[base + face_rows : base + each - 1, :] = got_ref[face_rows + capacity : last - 1, :]
        out_ref[base + each - 1 : base + each, :] = got_ref[last : last + 1, :]


def choose_kernel(
    samples, stators, blocks, wide_ref, peer_ref, block_ref, mapped_ref, mortar_ref, after_ref, out_ref, turned_ref
):
    mortar_high, mortar_low = split(mortar_ref[...])
    mortar_across = jnp.concatenate([mortar_high, mortar_high, mortar_low], 1)
    turned_ref[...] = dot_t(triple(mapped_ref[...]), mortar_across)
    rows = samples * blocks
    pairs = stators * QB
    wanted = (places_of(peer_ref, stators) * QB + block_ref[...]).astype(F32)
    wanted = jnp.broadcast_to(wanted, (8, rows)).astype(BF)
    lane = iota((rows, LANES), 1) % samples
    row = iota((rows, LANES), 0)
    spread = jnp.concatenate(
        [jnp.where(row == lane * blocks + b, 1.0, 0.0).astype(BF) for b in range(blocks)], 1
    )
    wanted = dot(wanted, spread)
    each = LANES // samples
    owner = (iota((samples, LANES), 1) // samples).astype(F32)
    for piece in range(2):
        values = wide_ref[piece * samples : (piece + 1) * samples, :].astype(F32)
        for b in range(blocks):
            want = jnp.broadcast_to(wanted[0:1, b * LANES : (b + 1) * LANES], (samples, LANES))
            for v in range(pairs // each):
                out_ref[(piece * blocks + b) * samples : (piece * blocks + b + 1) * samples,
                        v * LANES : (v + 1) * LANES] = jnp.where(want == owner + v * each, values, 0.0).astype(BF)


def element_kernel(
    face, rotor_start, table_ref, back_ref, coeffs_ref, rim_ref, edge_ref, curl_ref, jac_ref, fwd_ref, density_ref,
    adjoint_ref, rim_out_ref, grad_ref,
):
    samples, edges = coeffs_ref.shape
    elements = edge_ref.shape[1]
    table = table_ref[...]
    own_time = apply_table(table, coeffs_ref[...])
    rim_time = apply_table(table, rim_ref[:, :face])
    total = edges + face
    wides = -(-total // WIDE)
    whole = jnp.concatenate([own_time, rim_time], 1)
    extended = [whole[:, i * LANES : (i + 1) * LANES] for i in range(total // LANES)]
    padded = jnp.concatenate([whole, jnp.zeros((samples, wides * WIDE - total), F32)], 1)
    stack = jnp.concatenate(
        [part for w in range(wides) for part in split(padded[:, w * WIDE : (w + 1) * WIDE])], 0
    )
    places = iota((WIDE, LANES), 0).astype(F32).astype(BF)
    summed = jnp.zeros((wides * 2 * samples, WIDE), F32)
    for chunk in range(elements // CHUNK):
        lane_slices = [
            slice(chunk * CHUNK + half * LANES, chunk * CHUNK + (half + 1) * LANES) for half in range(CHUNK // LANES)
        ]
        rights = []
        for m in range(6):
            parts = []
            for lanes in lane_slices:
                index = edge_ref[m : m + 1, lanes]
                place = jnp.broadcast_to(index & (WIDE - 1), (16, LANES)).astype(F32).astype(BF)
                place = jnp.concatenate([place] * (WIDE // 16), 0)
                parts.append(jnp.where(place == places, jnp.ones_like(place), jnp.zeros_like(place)))
            rights.append(jnp.concatenate(parts, 1))
        looked = {m: dot(stack, rights[m]) for m in LOOK}
        left_lanes = [[] for _ in range(6)]
        for half, lanes in enumerate(lane_slices):
            at = slice(half * LANES, (half + 1) * LANES)
            values = []
            for m in range(6):
                index = edge_ref[m : m + 1, lanes]
                if m in LOOK:
                    found = [
                        looked[m][2 * w * samples : (2 * w + 1) * samples, at]
                        + looked[m][(2 * w + 1) * samples : (2 * w + 2) * samples, at]
                        for w in range(wides)
                    ]
                    high = jnp.broadcast_to(index // WIDE, (samples, LANES))
                else:
                    low = jnp.broadcast_to(index & (LANES - 1), (samples, LANES))
                    found = [
                        jnp.take_along_axis(part, low, axis=1, mode="promise_in_bounds") for part in extended
                    ]
                    high = jnp.broadcast_to(index // LANES, (samples, LANES))
                bit = 1
                while len(found) > 1:
                    odd = (high & bit) != 0
                    found = [
                        jnp.where(odd, found[i + 1], found[i]) if i + 1 < len(found) else found[i]
                        for i in range(0, len(found), 2)
                    ]
                    bit *= 2
                values.append(found[0])
            curl = [[curl_ref[c, m : m + 1, lanes] for m in range(6)] for c in range(3)]
            flux = []
            for c in range(3):
                acc = curl[c][0] * values[0]
                for m in range(1, 6):
                    acc = acc + curl[c][m] * values[m]
                flux.append(acc)
            energy = flux[0] * fwd_ref[0, :, lanes].astype(F32)
            for c in range(1, 3):
                energy = energy + flux[c] * fwd_ref[c, :, lanes].astype(F32)
            energy = jnp.sum(energy, 0, keepdims=True)
            density = density_ref[:, lanes]
            grad_ref[:, lanes] = SIMP_POWER * density * density * energy / samples
            jac = [jac_ref[k, :, lanes].astype(F32) for k in range(6)]
            field = [
                jac[0] * flux[0] + jac[3] * flux[1] + jac[4] * flux[2],
                jac[3] * flux[0] + jac[1] * flux[1] + jac[5] * flux[2],
                jac[4] * flux[0] + jac[5] * flux[1] + jac[2] * flux[2],
            ]
            for m in range(6):
                term = curl[0][m] * field[0] + curl[1][m] * field[1] + curl[2][m] * field[2]
                high, low = split(term)
                pair = jnp.concatenate([high, low], 0)
                index = edge_ref[m : m + 1, lanes]
                wide = jnp.broadcast_to(index // WIDE, (16, LANES)).astype(F32).astype(BF)
                wide = jnp.concatenate([wide] * (2 * samples // 16), 0)
                left_lanes[m].append(
                    jnp.concatenate([jnp.where(wide == w, pair, jnp.zeros_like(pair)) for w in range(wides)], 0)
                )
        left = jnp.concatenate([part for m in range(6) for part in left_lanes[m]], 1)
        summed = summed + dot_t(left, jnp.concatenate(rights, 1))
    pieces = []
    for w in range(wides):
        base = w * 2 * samples
        pieces.append(summed[base : base + samples] + summed[base + samples : base + 2 * samples])
    residual = jnp.concatenate(pieces, 1)
    own = jnp.concatenate(
        [residual[:, :rotor_start], residual[:, rotor_start:edges] + PENALTY * own_time[:, rotor_start:]], 1
    )
    back = back_ref[...]
    adjoint_ref[...] = apply_table(back, own)
    rim_out_ref[...] = apply_table(back, residual[:, edges:total])


def join_kernel(
    samples, stators, blocks, face, rotor_start, back_ref, adjoint_ref, rim_ref, turned_ref, choose_ref, *got_refs,
):
    *got_refs, out_ref = got_refs
    slots = 2 * samples * blocks
    capacity = slots // stators
    face_rows = QB * samples
    spots = got_spots(stators, face_rows, capacity)

    def got(p, part, count):
        start = spots[p][part]
        return got_refs[spots[p][0]][start : start + count, :]

    faces = jnp.concatenate([got(p, 1, face_rows) for p in range(stators)], 0)
    face_high, face_low = split(faces)
    facing = dot(choose_ref[...], jnp.concatenate([face_high, face_low], 1))
    rows = blocks * samples
    facing = (facing[:rows, :GE] + facing[:rows, GE:]) + (facing[rows:, :GE] + facing[rows:, GE:])

    lane = iota((1, LANES), 1)
    key_parts = []
    for v in range(slots // LANES):
        acc = jnp.zeros((1, LANES), F32)
        for p in range(v * LANES // capacity, (v + 1) * LANES // capacity):
            part = jnp.where(lane < capacity, got(p, 3, 1), 0.0)
            turn = p * capacity % LANES
            acc = acc + (pltpu.roll(part, turn, 1) if turn else part)
        key_parts.append(acc[0:1])
    key = jnp.concatenate(key_parts, 1)
    hit = jnp.where(key == (iota((face_rows, slots), 0) + 1).astype(F32), 1.0, 0.0)
    count = jnp.sum(hit, 1, keepdims=True)
    packed = jnp.concatenate([got(p, 2, capacity) for p in range(stators)], 0)
    packed_high, packed_low = split(packed)
    gathered = dot(hit.astype(BF), jnp.concatenate([packed_high, packed_low], 1))
    gathered = (gathered[:, :GE] + gathered[:, GE:] - count * turned_ref[...]) * (-PENALTY)
    stator_term = jnp.concatenate([gathered[q * samples : (q + 1) * samples] for q in range(QB)], 1)
    stator_term = apply_table(back_ref[...], stator_term)
    out_ref[:, :face] = adjoint_ref[:, :face] + rim_ref[...]
    out_ref[:, face : face + QB * GE] = adjoint_ref[:, face : face + QB * GE] + stator_term
    out_ref[:, face + QB * GE : rotor_start] = adjoint_ref[:, face + QB * GE : rotor_start]
    for b in range(blocks):
        at = slice(rotor_start + b * GE, rotor_start + (b + 1) * GE)
        out_ref[:, at] = adjoint_ref[:, at] + facing[b * samples : (b + 1) * samples]


def small(shape, kind):
    return math.prod(shape) * jnp.dtype(kind).itemsize <= NEAR_BYTES


def call(kernel, near, *shapes, far=(), scratch=()):
    def spec(inside, anywhere=False):
        if anywhere:
            return pl.BlockSpec(memory_space=pl.ANY)
        return pl.BlockSpec(memory_space=pltpu.VMEM) if inside else pl.BlockSpec()

    def run(*operands):
        close = [near and small(operand.shape, operand.dtype) for operand in operands]
        operands = [
            pltpu.with_memory_space_constraint(operand, pltpu.VMEM) if inside else operand
            for inside, operand in zip(close, operands)
        ]
        return pl.pallas_call(
            kernel,
            out_shape=[
                pltpu.VMEM(shape, kind) if inside and small(shape, kind) else jax.ShapeDtypeStruct(shape, kind)
                for inside, shape, kind in shapes
            ],
            in_specs=[spec(inside) for inside in close] + [spec(False, True)] * len(far),
            out_specs=[spec(inside and small(shape, kind)) for inside, shape, kind in shapes],
            scratch_shapes=scratch,
        )(*operands, *far)

    return run


def on_device(coeffs, elem_edge, curl_map, jacobian, flux_fwd, density, mortar, gap_peer, gap_block):
    stators = lax.axis_size("stator")
    samples, edges = coeffs.shape
    rows = gap_block.shape[0]
    blocks = rows // samples
    capacity = 2 * rows // stators
    face = edges // 8
    rotor_start = edges - blocks * GE
    elements = density.shape[0]
    face_rows = QB * samples
    table_value = dft_table(samples)
    table = jnp.asarray(table_parts(table_value))
    back = jnp.asarray(table_parts(table_value.T))
    wide = -PENALTY * table_value.T
    wide_high = wide.astype(BF)
    wide_low = (wide - wide_high.astype(np.float64)).astype(BF)
    wide = jnp.asarray(np.tile(np.concatenate([wide_high, wide_low], 0), (1, LANES // samples)))
    peer = gap_peer.reshape(1, rows)
    block = gap_block.reshape(1, rows)
    first = (table, coeffs, mortar, peer, block)
    later = (coeffs, elem_edge, density.reshape(1, elements), curl_map, flux_fwd, jacobian)
    each = face_rows + capacity + 1
    permutes = by_permutes(stators)
    if permutes:
        sends = [(True, (each, GE), F32)] * 2 + [(True, (each + capacity + 1, GE), F32)] * (stators // 2 - 1)
    else:
        sends = [(False, (stators * each, GE), F32)]

    def swapped(value, distance):
        return lax.ppermute(value, "stator", [(i, i ^ distance) for i in range(stators)])

    mapped, rim, *rest = call(
        functools.partial(gap_kernel, samples, stators, blocks, face, rotor_start, len(later)),
        False,
        (True, (face_rows, GE), F32),
        (True, (samples, face), F32),
        *[(True, value.shape, value.dtype) for value in later],
        *sends,
        far=first + later,
        scratch=[pltpu.VMEM(value.shape, value.dtype) for value in first]
        + [pltpu.SemaphoreType.DMA((len(first),)), pltpu.SemaphoreType.DMA((len(later),))],
    )()
    later, send = rest[: len(later)], rest[len(later) :]
    rim = shifted(rim, "axial", -1)
    if permutes:
        got = [send[0]]
        for i, value in enumerate(send[1:]):
            distance = max(1, 2 * i)
            got.append(swapped(value, distance))
    else:
        parts = send[0].reshape(stators, each, 1, GE)
        got = lax.all_to_all(parts, "stator", split_axis=0, concat_axis=0, tiled=True)
        got = [got.reshape(stators * each, GE)]
    own, edge, weight, curl, fwd, jac = later
    adjoint, rim_out, grad = call(
        functools.partial(element_kernel, face, rotor_start),
        True,
        (True, (samples, edges), F32),
        (True, (samples, face), F32),
        (False, (1, elements), F32),
    )(table, back, own, rim, edge, curl, jac, fwd, weight)
    if permutes:
        (send,) = call(
            functools.partial(relay_kernel, face_rows, capacity), True, (True, ((stators // 2 - 1) * each, GE), F32)
        )(*got[2:], rim_out)
        got.append(swapped(send, 1))
    lower = shifted(rim_out, "axial", 1)
    choose, turned = call(
        functools.partial(choose_kernel, samples, stators, blocks),
        True,
        (True, (2 * rows, stators * face_rows), BF),
        (True, (face_rows, GE), F32),
    )(wide, peer, block, mapped, mortar, rim_out)
    (adjoint,) = call(
        functools.partial(join_kernel, samples, stators, blocks, face, rotor_start),
        True,
        (False, (samples, edges), F32),
    )(back, adjoint, lower, turned, choose, *got)
    return adjoint, grad.reshape(elements)


def solution(mesh):
    placed = (
        P(None, ("stator", "axial")),
        P(None, ("stator", "axial")),
        P(None, None, ("stator", "axial")),
        P(None, None, ("stator", "axial")),
        P(None, None, ("stator", "axial")),
        P(("stator", "axial")),
        P(),
        P(("stator", "axial"), None),
        P(("stator", "axial")),
    )
    return jax.shard_map(
        on_device,
        mesh=mesh,
        in_specs=placed,
        out_specs=(P(None, ("stator", "axial")), P(("stator", "axial"))),
        check_vma=False,
    )
```

```python
import functools
import math

import jax
import jax.numpy as jnp
import numpy as np
from jax import lax
from jax.experimental import pallas as pl
from jax.experimental.pallas import tpu as pltpu
from jax.sharding import PartitionSpec as P

GE = 128
QB = 2
LANES = 128
WIDE = 256
CHUNK = 256
LOOK = (3, 5)
NEAR_BYTES = 1 << 20
MOST_PERMUTES = 8


PENALTY = 4.0
SIMP_POWER = 3.0

BF = jnp.bfloat16
F32 = jnp.float32


def shifted(value, axis, steps):
    count = lax.axis_size(axis)
    leading, last = (max(0, -steps), min(count, count - steps))
    return lax.ppermute(value, axis, [(source, source + steps) for source in range(leading, last)])


def dft_table(count):
    rows = np.arange(count, dtype=np.float64)[:, None]
    index = np.arange(count)
    harmonic = ((index + 1) // 2)[None, :]
    is_sine = ((index % 2 == 0) & (index > 0))[None, :]
    angle = 2.0 * math.pi * harmonic * rows / count
    return np.where(is_sine, np.sin(angle), np.cos(angle)) * math.sqrt(2.0 / count)


def table_parts(table):
    high = table.astype(BF)
    low = (table - high.astype(np.float64)).astype(BF)
    return np.concatenate([high, high, low, low], 1)


def split(value):
    high = value.astype(BF)
    low = (value - high.astype(F32)).astype(BF)
    return high, low


def dot(left, right):
    return jnp.dot(left, right, preferred_element_type=F32)


def dot_t(left, right):
    return lax.dot_general(left, right, (((1,), (1,)), ((), ())), preferred_element_type=F32)


def apply_table(table, value):
    high, low = split(value)
    return dot(table, jnp.concatenate([high, low, high, low], 0))


def iota(shape, dim):
    return lax.broadcasted_iota(jnp.int32, shape, dim)


def by_permutes(stators):
    return 4 <= stators <= MOST_PERMUTES and stators & (stators - 1) == 0


def places_of(peer_ref, stators):
    peers = peer_ref[...]
    return peers ^ lax.axis_index("stator") if by_permutes(stators) else peers


def triple(value):
    high, low = split(value)
    return jnp.concatenate([high, low, high], 1)


def gap_kernel(
    samples, stators, blocks, face, rotor_start, later, table_far, coeffs_far, mortar_far, peer_far, block_far, *refs,
):
    later_far, (mapped_ref, rim_ref), refs = refs[:later], refs[later : later + 2], refs[later + 2 :]
    later_near, refs = refs[:later], refs[later:]
    *send_refs, table_ref, coeffs_ref, mortar_ref, peer_ref, block_ref, sems, later_sems = refs
    fars = (peer_far, block_far, coeffs_far, table_far, mortar_far)
    nears = (peer_ref, block_ref, coeffs_ref, table_ref, mortar_ref)
    copies = [pltpu.make_async_copy(far, near, sems.at[i]) for i, (far, near) in enumerate(zip(fars, nears))]
    ahead = [pltpu.make_async_copy(far, near, later_sems.at[i]) for i, (far, near) in enumerate(zip(later_far, later_near))]
    for copy in copies + ahead:
        copy.start()
    rows = samples * blocks
    slots = 2 * rows
    capacity = slots // stators
    face_rows = QB * samples
    old, new = iota((rows, rows), 0), iota((rows, rows), 1)
    move = jnp.where(old == (new % samples) * blocks + new // samples, 1.0, 0.0).astype(BF)
    earlier = jnp.where(old < new, 1.0, 0.0)
    slot = iota((slots, rows), 0).astype(F32)
    sample = (iota((1, rows), 1) % samples).astype(F32) + 1.0
    for copy in copies:
        copy.wait()
    both = jnp.concatenate([places_of(peer_ref, stators), block_ref[...]], 0).astype(F32)
    both = jnp.concatenate([both, jnp.zeros((6, rows), F32)], 0).astype(BF)
    both = dot(both, move)
    peers, chosen = both[0:1], both[1:2]
    rim_ref[...] = coeffs_ref[:, :face]
    table = table_ref[...]
    rotor_time = apply_table(table, coeffs_ref[:, rotor_start : rotor_start + blocks * GE])
    face_time = apply_table(table, coeffs_ref[:, face : face + QB * GE])
    rotors = jnp.concatenate([rotor_time[:, b * GE : (b + 1) * GE] for b in range(blocks)], 0)
    faces = jnp.concatenate([face_time[:, q * GE : (q + 1) * GE] for q in range(QB)], 0)
    mortar_high, mortar_low = split(mortar_ref[...])
    mortar_down = jnp.concatenate([mortar_high, mortar_high, mortar_low], 0)
    mortar_across = jnp.concatenate([mortar_high, mortar_high, mortar_low], 1)
    rotor_turned = dot_t(triple(rotors), mortar_across)
    mapped = dot(triple(faces), mortar_down)
    mapped_ref[...] = mapped
    across = jnp.broadcast_to(peers, (rows, rows))
    down = jnp.transpose(across)
    rank = jnp.sum(jnp.where(across == down, earlier, 0.0), 0, keepdims=True)
    place = peers * capacity + rank
    pick = jnp.where(slot == place, 1.0, 0.0).astype(BF)
    rotor_high, rotor_low = split(rotor_turned)
    picked = dot(pick, jnp.concatenate([rotor_high, rotor_low], 1))
    packed = picked[:, :GE] + picked[:, GE:]
    key = chosen * samples + sample
    keys = dot_t(jnp.broadcast_to(key, (8, rows)).astype(BF), pick)
    spots = send_spots(stators, face_rows, capacity)
    for p in range(stators):
        start = p * capacity
        part = keys[:, start // LANES * LANES : (start // LANES + 1) * LANES]
        turn = (LANES - start % LANES) % LANES
        if turn:
            part = pltpu.roll(part, turn, 1)
        which, face_at, slot_at, key_at = spots[p]
        if face_at is not None:
            send_refs[which][face_at : face_at + face_rows, :] = mapped
        send_refs[which][slot_at : slot_at + capacity, :] = packed[start : start + capacity]
        send_refs[which][key_at : key_at + 1, :] = part[:1]
    for copy in ahead:
        copy.wait()


def send_spots(stators, face_rows, capacity):
    each = face_rows + capacity + 1
    if not by_permutes(stators):
        return [(0, p * each, p * each + face_rows, (p + 1) * each - 1) for p in range(stators)]
    spots = [(0, 0, face_rows, each - 1), (1, 0, face_rows, each - 1)]
    for p in range(2, stators, 2):
        last = face_rows + 2 * capacity
        spots.append((1 + p // 2, 0, face_rows, last))
        spots.append((1 + p // 2, None, face_rows + capacity, last + 1))
    return spots


def got_spots(stators, face_rows, capacity):
    each = face_rows + capacity + 1
    spots = send_spots(stators, face_rows, capacity)
    if by_permutes(stators):
        for p in range(3, stators, 2):
            base = (p - 3) // 2 * each
            spots[p] = (1 + stators // 2, base, base + face_rows, base + each - 1)
    return spots


def relay_kernel(face_rows, capacity, *refs):
    *got_refs, after_ref, out_ref = refs
    each = face_rows + capacity + 1
    last = face_rows + 2 * capacity + 1
    for i, got_ref in enumerate(got_refs):
        base = i * each
        out_ref[base : base + face_rows, :] = got_ref[:face_rows, :]
        out_ref[base + face_rows : base + each - 1, :] = got_ref[face_rows + capacity : last - 1, :]
        out_ref[base + each - 1 : base + each, :] = got_ref[last : last + 1, :]


def choose_kernel(
    samples, stators, blocks, wide_ref, peer_ref, block_ref, mapped_ref, mortar_ref, after_ref, out_ref, turned_ref
):
    mortar_high, mortar_low = split(mortar_ref[...])
    mortar_across = jnp.concatenate([mortar_high, mortar_high, mortar_low], 1)
    turned_ref[...] = dot_t(triple(mapped_ref[...]), mortar_across)
    rows = samples * blocks
    pairs = stators * QB
    wanted = (places_of(peer_ref, stators) * QB + block_ref[...]).astype(F32)
    wanted = jnp.broadcast_to(wanted, (8, rows)).astype(BF)
    lane = iota((rows, LANES), 1) % samples
    row = iota((rows, LANES), 0)
    spread = jnp.concatenate(
        [jnp.where(row == lane * blocks + b, 1.0, 0.0).astype(BF) for b in range(blocks)], 1
    )
    wanted = dot(wanted, spread)
    each = LANES // samples
    owner = (iota((samples, LANES), 1) // samples).astype(F32)
    for piece in range(2):
        values = wide_ref[piece * samples : (piece + 1) * samples, :].astype(F32)
        for b in range(blocks):
            want = jnp.broadcast_to(wanted[0:1, b * LANES : (b + 1) * LANES], (samples, LANES))
            for v in range(pairs // each):
                out_ref[(piece * blocks + b) * samples : (piece * blocks + b + 1) * samples,
                        v * LANES : (v + 1) * LANES] = jnp.where(want == owner + v * each, values, 0.0).astype(BF)


def element_kernel(
    face, rotor_start, table_ref, back_ref, coeffs_ref, rim_ref, edge_ref, curl_ref, jac_ref, fwd_ref, density_ref,
    adjoint_ref, rim_out_ref, grad_ref,
):
    samples, edges = coeffs_ref.shape
    elements = edge_ref.shape[1]
    table = table_ref[...]
    own_time = apply_table(table, coeffs_ref[...])
    rim_time = apply_table(table, rim_ref[:, :face])
    total = edges + face
    wides = -(-total // WIDE)
    whole = jnp.concatenate([own_time, rim_time], 1)
    extended = [whole[:, i * LANES : (i + 1) * LANES] for i in range(total // LANES)]
    padded = jnp.concatenate([whole, jnp.zeros((samples, wides * WIDE - total), F32)], 1)
    stack = jnp.concatenate(
        [part for w in range(wides) for part in split(padded[:, w * WIDE : (w + 1) * WIDE])], 0
    )
    places = iota((WIDE, LANES), 0).astype(F32).astype(BF)
    summed = jnp.zeros((wides * 2 * samples, WIDE), F32)

    def prepare(chunk):
        lane_slices = [
            slice(chunk * CHUNK + half * LANES, chunk * CHUNK + (half + 1) * LANES) for half in range(CHUNK // LANES)
        ]
        rights = []
        for m in range(6):
            parts = []
            for lanes in lane_slices:
                index = edge_ref[m : m + 1, lanes]
                place = jnp.broadcast_to(index & (WIDE - 1), (16, LANES)).astype(F32).astype(BF)
                place = jnp.concatenate([place] * (WIDE // 16), 0)
                parts.append(jnp.where(place == places, jnp.ones_like(place), jnp.zeros_like(place)))
            rights.append(jnp.concatenate(parts, 1))
        looked = {m: dot(stack, rights[m]) for m in LOOK}
        return lane_slices, rights, looked

    chunks = elements // CHUNK
    ready = [prepare(chunk) for chunk in range(min(1, chunks))]
    waiting = []
    for chunk in range(chunks):
        if chunk + 1 < chunks and 1:
            ready.append(prepare(chunk + 1))
        lane_slices, rights, looked = ready[chunk]
        left_lanes = [[] for _ in range(6)]
        for half, lanes in enumerate(lane_slices):
            at = slice(half * LANES, (half + 1) * LANES)
            values = []
            for m in range(6):
                index = edge_ref[m : m + 1, lanes]
                if m in LOOK:
                    found = [
                        looked[m][2 * w * samples : (2 * w + 1) * samples, at]
                        + looked[m][(2 * w + 1) * samples : (2 * w + 2) * samples, at]
                        for w in range(wides)
                    ]
                    high = jnp.broadcast_to(index // WIDE, (samples, LANES))
                else:
                    low = jnp.broadcast_to(index & (LANES - 1), (samples, LANES))
                    found = [
                        jnp.take_along_axis(part, low, axis=1, mode="promise_in_bounds") for part in extended
                    ]
                    high = jnp.broadcast_to(index // LANES, (samples, LANES))
                bit = 1
                while len(found) > 1:
                    odd = (high & bit) != 0
                    found = [
                        jnp.where(odd, found[i + 1], found[i]) if i + 1 < len(found) else found[i]
                        for i in range(0, len(found), 2)
                    ]
                    bit *= 2
                values.append(found[0])
            curl = [[curl_ref[c, m : m + 1, lanes] for m in range(6)] for c in range(3)]
            flux = []
            for c in range(3):
                acc = curl[c][0] * values[0]
                for m in range(1, 6):
                    acc = acc + curl[c][m] * values[m]
                flux.append(acc)
            energy = flux[0] * fwd_ref[0, :, lanes].astype(F32)
            for c in range(1, 3):
                energy = energy + flux[c] * fwd_ref[c, :, lanes].astype(F32)
            energy = jnp.sum(energy, 0, keepdims=True)
            density = density_ref[:, lanes]
            grad_ref[:, lanes] = SIMP_POWER * density * density * energy / samples
            jac = [jac_ref[k, :, lanes].astype(F32) for k in range(6)]
            field = [
                jac[0] * flux[0] + jac[3] * flux[1] + jac[4] * flux[2],
                jac[3] * flux[0] + jac[1] * flux[1] + jac[5] * flux[2],
                jac[4] * flux[0] + jac[5] * flux[1] + jac[2] * flux[2],
            ]
            for m in range(6):
                term = curl[0][m] * field[0] + curl[1][m] * field[1] + curl[2][m] * field[2]
                high, low = split(term)
                pair = jnp.concatenate([high, low], 0)
                index = edge_ref[m : m + 1, lanes]
                wide = jnp.broadcast_to(index // WIDE, (16, LANES)).astype(F32).astype(BF)
                wide = jnp.concatenate([wide] * (2 * samples // 16), 0)
                left_lanes[m].append(
                    jnp.concatenate([jnp.where(wide == w, pair, jnp.zeros_like(pair)) for w in range(wides)], 0)
                )
        left = jnp.concatenate([part for m in range(6) for part in left_lanes[m]], 1)
        waiting.append((left, jnp.concatenate(rights, 1)))
        if chunk:
            summed = summed + dot_t(*waiting[chunk - 1])
    summed = summed + dot_t(*waiting[-1])
    pieces = []
    for w in range(wides):
        base = w * 2 * samples
        pieces.append(summed[base : base + samples] + summed[base + samples : base + 2 * samples])
    residual = jnp.concatenate(pieces, 1)
    own = jnp.concatenate(
        [residual[:, :rotor_start], residual[:, rotor_start:edges] + PENALTY * own_time[:, rotor_start:]], 1
    )
    back = back_ref[...]
    adjoint_ref[...] = apply_table(back, own)
    rim_out_ref[...] = apply_table(back, residual[:, edges:total])


def join_kernel(
    samples, stators, blocks, face, rotor_start, back_ref, adjoint_ref, rim_ref, turned_ref, choose_ref, *got_refs,
):
    *got_refs, out_ref = got_refs
    slots = 2 * samples * blocks
    capacity = slots // stators
    face_rows = QB * samples
    spots = got_spots(stators, face_rows, capacity)

    def got(p, part, count):
        start = spots[p][part]
        return got_refs[spots[p][0]][start : start + count, :]

    faces = jnp.concatenate([got(p, 1, face_rows) for p in range(stators)], 0)
    face_high, face_low = split(faces)
    facing = dot(choose_ref[...], jnp.concatenate([face_high, face_low], 1))
    rows = blocks * samples
    facing = (facing[:rows, :GE] + facing[:rows, GE:]) + (facing[rows:, :GE] + facing[rows:, GE:])

    lane = iota((1, LANES), 1)
    key_parts = []
    for v in range(slots // LANES):
        acc = jnp.zeros((1, LANES), F32)
        for p in range(v * LANES // capacity, (v + 1) * LANES // capacity):
            part = jnp.where(lane < capacity, got(p, 3, 1), 0.0)
            turn = p * capacity % LANES
            acc = acc + (pltpu.roll(part, turn, 1) if turn else part)
        key_parts.append(acc[0:1])
    key = jnp.concatenate(key_parts, 1)
    hit = jnp.where(key == (iota((face_rows, slots), 0) + 1).astype(F32), 1.0, 0.0)
    count = jnp.sum(hit, 1, keepdims=True)
    packed = jnp.concatenate([got(p, 2, capacity) for p in range(stators)], 0)
    packed_high, packed_low = split(packed)
    gathered = dot(hit.astype(BF), jnp.concatenate([packed_high, packed_low], 1))
    gathered = (gathered[:, :GE] + gathered[:, GE:] - count * turned_ref[...]) * (-PENALTY)
    stator_term = jnp.concatenate([gathered[q * samples : (q + 1) * samples] for q in range(QB)], 1)
    stator_term = apply_table(back_ref[...], stator_term)
    out_ref[:, :face] = adjoint_ref[:, :face] + rim_ref[...]
    out_ref[:, face : face + QB * GE] = adjoint_ref[:, face : face + QB * GE] + stator_term
    out_ref[:, face + QB * GE : rotor_start] = adjoint_ref[:, face + QB * GE : rotor_start]
    for b in range(blocks):
        at = slice(rotor_start + b * GE, rotor_start + (b + 1) * GE)
        out_ref[:, at] = adjoint_ref[:, at] + facing[b * samples : (b + 1) * samples]


def small(shape, kind):
    return math.prod(shape) * jnp.dtype(kind).itemsize <= NEAR_BYTES


def call(kernel, near, *shapes, far=(), scratch=()):
    def spec(inside, anywhere=False):
        if anywhere:
            return pl.BlockSpec(memory_space=pl.ANY)
        return pl.BlockSpec(memory_space=pltpu.VMEM) if inside else pl.BlockSpec()

    def run(*operands):
        close = [near and small(operand.shape, operand.dtype) for operand in operands]
        operands = [
            pltpu.with_memory_space_constraint(operand, pltpu.VMEM) if inside else operand
            for inside, operand in zip(close, operands)
        ]
        return pl.pallas_call(
            kernel,
            out_shape=[
                pltpu.VMEM(shape, kind) if inside and small(shape, kind) else jax.ShapeDtypeStruct(shape, kind)
                for inside, shape, kind in shapes
            ],
            in_specs=[spec(inside) for inside in close] + [spec(False, True)] * len(far),
            out_specs=[spec(inside and small(shape, kind)) for inside, shape, kind in shapes],
            scratch_shapes=scratch,
        )(*operands, *far)

    return run


def on_device(coeffs, elem_edge, curl_map, jacobian, flux_fwd, density, mortar, gap_peer, gap_block):
    stators = lax.axis_size("stator")
    samples, edges = coeffs.shape
    rows = gap_block.shape[0]
    blocks = rows // samples
    capacity = 2 * rows // stators
    face = edges // 8
    rotor_start = edges - blocks * GE
    elements = density.shape[0]
    face_rows = QB * samples
    table_value = dft_table(samples)
    table = jnp.asarray(table_parts(table_value))
    back = jnp.asarray(table_parts(table_value.T))
    wide = -PENALTY * table_value.T
    wide_high = wide.astype(BF)
    wide_low = (wide - wide_high.astype(np.float64)).astype(BF)
    wide = jnp.asarray(np.tile(np.concatenate([wide_high, wide_low], 0), (1, LANES // samples)))
    peer = gap_peer.reshape(1, rows)
    block = gap_block.reshape(1, rows)
    first = (table, coeffs, mortar, peer, block)
    later = (coeffs, elem_edge, density.reshape(1, elements), curl_map, flux_fwd, jacobian)
    each = face_rows + capacity + 1
    permutes = by_permutes(stators)
    if permutes:
        sends = [(True, (each, GE), F32)] * 2 + [(True, (each + capacity + 1, GE), F32)] * (stators // 2 - 1)
    else:
        sends = [(False, (stators * each, GE), F32)]

    def swapped(value, distance):
        return lax.ppermute(value, "stator", [(i, i ^ distance) for i in range(stators)])

    mapped, rim, *rest = call(
        functools.partial(gap_kernel, samples, stators, blocks, face, rotor_start, len(later)),
        False,
        (True, (face_rows, GE), F32),
        (True, (samples, face), F32),
        *[(True, value.shape, value.dtype) for value in later],
        *sends,
        far=first + later,
        scratch=[pltpu.VMEM(value.shape, value.dtype) for value in first]
        + [pltpu.SemaphoreType.DMA((len(first),)), pltpu.SemaphoreType.DMA((len(later),))],
    )()
    later, send = rest[: len(later)], rest[len(later) :]
    rim = shifted(rim, "axial", -1)
    if permutes:
        got = [send[0]]
        for i, value in enumerate(send[1:]):
            distance = max(1, 2 * i)
            got.append(swapped(value, distance))
    else:
        parts = send[0].reshape(stators, each, 1, GE)
        got = lax.all_to_all(parts, "stator", split_axis=0, concat_axis=0, tiled=True)
        got = [got.reshape(stators * each, GE)]
    own, edge, weight, curl, fwd, jac = later
    adjoint, rim_out, grad = call(
        functools.partial(element_kernel, face, rotor_start),
        True,
        (True, (samples, edges), F32),
        (True, (samples, face), F32),
        (False, (1, elements), F32),
    )(table, back, own, rim, edge, curl, jac, fwd, weight)
    if permutes:
        (send,) = call(
            functools.partial(relay_kernel, face_rows, capacity), True, (True, ((stators // 2 - 1) * each, GE), F32)
        )(*got[2:], rim_out)
        got.append(swapped(send, 1))
    lower = shifted(rim_out, "axial", 1)
    choose, turned = call(
        functools.partial(choose_kernel, samples, stators, blocks),
        True,
        (True, (2 * rows, stators * face_rows), BF),
        (True, (face_rows, GE), F32),
    )(wide, peer, block, mapped, mortar, rim_out)
    (adjoint,) = call(
        functools.partial(join_kernel, samples, stators, blocks, face, rotor_start),
        True,
        (False, (samples, edges), F32),
    )(back, adjoint, lower, turned, choose, *got)
    return adjoint, grad.reshape(elements)


def solution(mesh):
    placed = (
        P(None, ("stator", "axial")),
        P(None, ("stator", "axial")),
        P(None, None, ("stator", "axial")),
        P(None, None, ("stator", "axial")),
        P(None, None, ("stator", "axial")),
        P(("stator", "axial")),
        P(),
        P(("stator", "axial"), None),
        P(("stator", "axial")),
    )
    return jax.shard_map(
        on_device,
        mesh=mesh,
        in_specs=placed,
        out_specs=(P(None, ("stator", "axial")), P(("stator", "axial"))),
        check_vma=False,
    )
```
